768 devices in a mesh: section: 3 (over z_lo), win: 64 (over x, y, core), dp: 4 (over z_hi).
Axes of the slice: x: 4, y: 8, z: 12 (z_hi: 4, z_lo: 3; z = z_hi * 3 + z_lo), core: 2. Of those that a mesh axis runs over, the one named last changes fastest.
Arguments:
- tokens: bfloat16 [2, 64, 4, 64, 1536], P(None, 'win', 'dp'), may hold values from -6 to 6
- regions: int32 [3, 64, 256], P('section', 'win'), may hold values from 0 to 3
- norm_gain: float32 [3, 1536], P('section'), may hold values from 0.1 to 1.9
- qkv_weight: bfloat16 [3, 1536, 3, 1024], P('section', None, None, 'dp'), as said below
- out_weight: bfloat16 [3, 1024, 1536], P('section', 'dp'), may hold values from -2 to 2
- final_gain: float32 [1536], replicated, may hold values from 0.1 to 1.9
- dec_weight: bfloat16 [1536, 1104], P(None, 'section'), may hold values from -0.15625 to 0.15625
Outputs:
- decoded: bfloat16 [2, 64, 4, 64, 1104], P(None, 'win', 'dp', None, 'section')
The draws below stay inside these ranges and needn't reach their ends.
Inputs may be any that keep to these rules, and one draw needn't show every extreme that they name: `qkv_weight`: entries lie below 80 / sqrt(1536) in magnitude.
All inputs are finite; a program needn't handle non-finite values.
Results may differ from the reference program's by a relative error of at most 0.03.
Values may be sent and summed in bfloat16 or wider, within the bound.
No kernel may reach another device: no remote copies, remote signals or barrier semaphores. Data moves between devices by JAX's collectives and lax.ppermute only.
A program may use at most 32 MiB of HBM per device.

```python
import math
import jax
import jax.numpy as jnp
import numpy as np
from jax import lax

D = 1536
HEADS = 16
HEAD_DIM = 64
DEC = 1104
QUAD = 64
MICRO = 2
LAYERS = 3
WINDOWS = 64


def draw_qkv_weight(key, part):
    parts_keys = jax.random.split(key, 1)
    shape = (LAYERS, D, 3, HEADS, HEAD_DIM)
    full = jax.random.truncated_normal(parts_keys[0], -4.0, 4.0, shape, jnp.float32) / math.sqrt(D)
    return full.reshape(LAYERS, D, 3, HEADS * HEAD_DIM).astype(jnp.bfloat16)


def set_ends(entries, rng, smallest, high):
    longest = entries.shape.index(max(entries.shape))
    spots = []
    for shift in (0, 1):
        where = [jax.random.randint(jax.random.fold_in(rng, axis), (), 0, length) for axis, length in enumerate(entries.shape)]
        where[longest] = (where[longest] + shift) % entries.shape[longest]
        spots.append(tuple(where))
    return entries.at[spots[0]].set(smallest).at[spots[1]].set(high)


def steps_of(key, dims, shards, smallest, high):
    def one(axis_at, blocks):
        steps = jax.random.uniform(jax.random.fold_in(jax.random.fold_in(key, 6), axis_at), (blocks,), jnp.float32, smallest / len(shards), high / len(shards))
        return jnp.repeat(jnp.exp(steps), dims[axis_at] // blocks).reshape((-1,) + (1,) * (len(dims) - axis_at - 1))

    gain = one(*shards[0])
    for cut in shards[1:]:
        gain = gain * one(*cut)
    return gain


def rank_bounds(count, skew):
    weights = [(1 << 20) // math.isqrt(grade ** skew) + 1 for grade in range(1, count + 1)]
    width = 1 + sum(weights) // (1 << 30)
    return np.cumsum(np.array([max(1, weight // width) for weight in weights]))


def skewed_ids(key, shape, amount, slope):
    listing = rank_bounds(amount, slope)
    pick = jax.random.randint(jax.random.fold_in(key, 1), shape, 0, int(listing[amount - 1]))
    grade = jnp.searchsorted(jnp.asarray(listing, jnp.int32), pick, side="right")
    return jax.random.permutation(jax.random.fold_in(key, 2), amount)[grade].astype(jnp.int32)


def normal_values(stream_key, shape, width, reach, shards=(), kind=jnp.bfloat16):
    values = jax.random.normal(stream_key, shape, jnp.float32) * width
    if len(shards) > 0:
        values = steps_of(stream_key, shape, shards, -0.22, 0.18) * values
    return jnp.clip(values, min=-reach, max=reach).astype(kind)


def setup_inputs(seed: int = 0) -> dict:
    streams_of = jax.random.split(jax.random.key(seed), 8)
    return {
        "tokens": normal_values(streams_of[0], (MICRO, WINDOWS, 4, QUAD, D), 1.0, 6.0, ((1, 64), (2, 4))),
        "regions": set_ends(skewed_ids(streams_of[1], (LAYERS, WINDOWS, 4 * QUAD), 4, 2), jax.random.fold_in(streams_of[1], 3), 0, 3).astype(jnp.int32),
        "norm_gain": jnp.clip(1.0 + 0.18 * jax.random.normal(streams_of[2], (LAYERS, D), jnp.float32), 0.1, 1.9),
        "qkv_weight": draw_qkv_weight(jax.random.fold_in(streams_of[7], 71), 0),
        "out_weight": normal_values(streams_of[4], (LAYERS, HEADS * HEAD_DIM, D), 0.15, 2.0, ((0, 3), (1, 4))),
        "final_gain": jnp.clip(1.0 + 0.18 * jax.random.normal(streams_of[5], (D,), jnp.float32), 0.1, 1.9),
        "dec_weight": normal_values(streams_of[6], (D, DEC), D ** -0.5, 0.15625, ((1, 3),)),
    }


def normalize(hidden, scales):
    values = hidden.astype(jnp.float32)
    center = values - lax.optimization_barrier(jnp.mean(values, axis=-1, keepdims=True))
    spread = lax.optimization_barrier(jnp.mean(center * center, axis=-1, keepdims=True))
    return (center * lax.rsqrt(spread + 1e-05) * scales).astype(jnp.bfloat16)

def rounded(values):
    return lax.optimization_barrier(values.astype(jnp.bfloat16)).astype(jnp.float32)

def attend(projected, labels):
    row_count = projected.shape[0]
    queries = projected[:, 0].reshape(row_count, HEADS, HEAD_DIM).astype(jnp.float32)
    keys_all = projected[:, 1].reshape(row_count, HEADS, HEAD_DIM).astype(jnp.float32)
    values_all = projected[:, 2].reshape(row_count, HEADS, HEAD_DIM).astype(jnp.float32)
    scores = jnp.einsum('qhe,khe->hqk', queries, keys_all) / jnp.sqrt(jnp.float32(HEAD_DIM))
    allowed = labels[:, None] == labels[None, :]
    scores = jnp.where(allowed[None], scores, -jnp.inf)
    largest = lax.optimization_barrier(jnp.max(scores, axis=-1, keepdims=True))
    weights = jnp.exp(scores - largest)
    shares = (weights / lax.optimization_barrier(jnp.sum(weights, axis=-1, keepdims=True))).astype(jnp.bfloat16)
    blended = jnp.einsum('hqk,khe->qhe', shares.astype(jnp.float32), values_all)
    return blended.astype(jnp.bfloat16).reshape(row_count, HEADS * HEAD_DIM)

def reference(tokens, regions, norm_gain, qkv_weight, out_weight, final_gain, dec_weight):
    windows = tokens.shape[1]
    block = HEADS * HEAD_DIM // 4
    half = QUAD // 2

    def layer(hidden, labels_all, scales, projection, out_matrix):
        normed = normalize(hidden, scales).reshape(windows, 4 * QUAD, D)
        projected = jnp.einsum('wtd,dcf->wtcf', normed.astype(jnp.float32), projection.astype(jnp.float32)).astype(jnp.bfloat16)

        def one_window(items):
            window_proj, labels = items
            blended = attend(window_proj, labels)
            total = jnp.zeros((4 * QUAD, D), jnp.float32)
            for source in range(4):
                total = total + rounded(jnp.dot(blended[:, source * block:(source + 1) * block], out_matrix[source * block:(source + 1) * block], preferred_element_type=jnp.float32))
            return total
        update = lax.map(one_window, (projected, labels_all))
        return (hidden.astype(jnp.float32) + update.reshape(windows, 4, QUAD, D)).astype(jnp.bfloat16)
    outputs = []
    for micro_index in range(MICRO):
        hidden = tokens[micro_index]
        for layer_index in range(LAYERS):
            hidden = layer(hidden, regions[layer_index], norm_gain[layer_index], qkv_weight[layer_index], out_weight[layer_index])
            hidden = jnp.concatenate([hidden[:, :, half:], jnp.roll(hidden[:, :, :half], -1, axis=0)], axis=2)
        final = normalize(hidden, final_gain)
        result = jnp.dot(final.reshape(-1, D), dec_weight, preferred_element_type=jnp.float32)
        outputs.append(result.astype(jnp.bfloat16).reshape(windows, 4, QUAD, DEC))
    return jnp.stack(outputs)
```

```python
import jax
import jax.numpy as jnp
import numpy as np
from jax import lax
from jax.experimental import pallas as pl
from jax.experimental.pallas import tpu as pltpu
from jax.sharding import Mesh
from jax.sharding import PartitionSpec as P

HEAD = 64
AXES = ("section", "x", "y", "core", "dp")
WIN = ("x", "y", "core")


def chip_of(parity, micro):
    return 2 * micro + (parity ^ micro)


def parity_of(chip):
    return (chip ^ (chip >> 1)) & 1


def norm(values, gain):
    center = values - jnp.mean(values, axis=-1, keepdims=True)
    spread = jnp.mean(center * center, axis=-1, keepdims=True)
    return (center * lax.rsqrt(spread + 1e-05) * gain).astype(jnp.bfloat16)


def layer_kernel(lq, lk, gain, own_a, own_b, far_a, far_b, native, others, out_a, out_b, held, normed, acc, sems):
    quarters = held.shape[0]
    slices, per, width = held.shape[1:]
    inner = width // 3
    rows = per * 3 // 4
    orows = per // 8
    copies = [pltpu.make_async_copy(native, held.at[0], sems.at[0])]
    for step in range(1, quarters):
        copies.append(pltpu.make_async_copy(others.at[:, step - 1], held.at[step], sems.at[step]))
    for copy in copies:
        copy.start()
    part = own_a.shape[0]
    half = 2 * part
    for index, ref in enumerate((own_a, own_b, far_a, far_b)):
        normed[index * part:(index + 1) * part, :] = norm(ref[...].astype(jnp.float32), gain[...])
    allowed = lq[...] == lk[...]
    for step in range(quarters):
        copies[step].wait()
        weight = held[step, :, :rows, :].reshape(slices * rows, width)
        keyval = jnp.dot(normed[...], weight[:, inner:], preferred_element_type=jnp.float32).astype(jnp.bfloat16)
        query = jnp.dot(normed[:half, :], weight[:, :inner], preferred_element_type=jnp.float32).astype(jnp.bfloat16)
        parts = []
        for head in range(inner // HEAD):
            at = head * HEAD
            scores = lax.dot_general(
                query[:, at:at + HEAD], keyval[:, at:at + HEAD],
                (((1,), (1,)), ((), ())), preferred_element_type=jnp.float32,
            ) * (HEAD ** -0.5)
            scores = jnp.where(allowed, scores, -jnp.inf)
            weights = jnp.exp(scores - jnp.max(scores, axis=-1, keepdims=True))
            shares = (weights / jnp.sum(weights, axis=-1, keepdims=True)).astype(jnp.bfloat16)
            parts.append(jnp.dot(shares, keyval[:, inner + at:inner + at + HEAD], preferred_element_type=jnp.float32))
        blended = jnp.concatenate(parts, axis=-1).astype(jnp.bfloat16)
        for side in range(2):
            low = rows + side * orows
            matrix = held[step, :, low:low + orows, :].reshape(slices * orows, width)
            update = jnp.dot(blended, matrix, preferred_element_type=jnp.float32).astype(jnp.bfloat16).astype(jnp.float32)
            cols = slice(side * width, (side + 1) * width)
            if step == 0:
                acc[:, cols] = update
            else:
                acc[:, cols] += update
    out_a[...] = (own_a[...].astype(jnp.float32) + acc[:part, :]).astype(jnp.bfloat16)
    out_b[...] = (own_b[...].astype(jnp.float32) + acc[part:, :]).astype(jnp.bfloat16)


def layer(lq, lk, gain, own_a, own_b, far_a, far_b, native, others):
    part, depth = own_a.shape
    quarters = others.shape[1] + 1
    vmem = pl.BlockSpec(memory_space=pltpu.VMEM)
    hbm = pl.BlockSpec(memory_space=pl.ANY)
    shape = jax.ShapeDtypeStruct((part, depth), jnp.bfloat16)
    return pl.pallas_call(
        layer_kernel,
        out_shape=(shape, shape),
        in_specs=[vmem] * 7 + [hbm] * 2,
        out_specs=(vmem, vmem),
        scratch_shapes=[
            pltpu.VMEM((quarters,) + native.shape, jnp.bfloat16),
            pltpu.VMEM((4 * part, depth), jnp.bfloat16),
            pltpu.VMEM((2 * part, depth), jnp.float32),
            pltpu.SemaphoreType.DMA((quarters,)),
        ],
        compiler_params=pltpu.CompilerParams(vmem_limit_bytes=40 << 20),
        cost_estimate=pl.CostEstimate(flops=2_600_000_000, bytes_accessed=14_000_000, transcendentals=524288),
        name="layer",
    )(lq, lk, gain, own_a, own_b, far_a, far_b, native, others)


def decode_kernel(gain, part_a, part_b, matrix, out):
    rows = jnp.concatenate([part_a[...], part_b[...]], axis=0).astype(jnp.float32)
    final = norm(rows, gain[...])
    slices, sections, per, width = matrix.shape
    for section in range(sections):
        weight = matrix[:, section].reshape(slices * per, width)
        out[section] = jnp.dot(final, weight, preferred_element_type=jnp.float32).astype(jnp.bfloat16)


def decode(gain, part_a, part_b, matrix):
    vmem = pl.BlockSpec(memory_space=pltpu.VMEM)
    return pl.pallas_call(
        decode_kernel,
        out_shape=jax.ShapeDtypeStruct((matrix.shape[1], 2 * part_a.shape[0], matrix.shape[3]), jnp.bfloat16),
        in_specs=[vmem] * 4,
        out_specs=vmem,
        compiler_params=pltpu.CompilerParams(vmem_limit_bytes=24 << 20),
        cost_estimate=pl.CostEstimate(flops=450_000_000, bytes_accessed=4_500_000, transcendentals=0),
        name="decode",
    )(gain, part_a, part_b, matrix)


def solution(mesh):
    sections, windows, bands = (mesh.shape[name] for name in ("section", "win", "dp"))
    fine = Mesh(np.asarray(mesh.devices).reshape(sections, windows // 16, 8, 2, bands), AXES)
    chips = windows // 2

    def place(section, window, chip):
        return (section * windows + window % windows) * bands + chip

    def send(value, route, sources):
        pairs = []
        for section in sources:
            for window in range(windows):
                for chip in range(bands):
                    target = route(section, window, chip)
                    if target is not None:
                        pairs.append((place(section, window, chip), place(*target)))
        return lax.ppermute(value, AXES, pairs)

    def to_other_core(value, sources):
        return send(value, lambda s, w, d: (s, w ^ 1, d), sources)

    def body(tokens, regions, norm_gain, qkv_weight, out_weight, final_gain, dec_weight):
        section = lax.axis_index("section")
        core = lax.axis_index("core")
        chip = lax.axis_index("dp")
        mine = lax.axis_index("y") * 2 + core
        depth = tokens.shape[-1]
        quad = tokens.shape[3]
        half = quad // 2
        micro = chip >> 1
        parity = (chip ^ (chip >> 1)) & 1
        width = qkv_weight.shape[2] * qkv_weight.shape[3]

        native = jnp.concatenate(
            [
                qkv_weight[0].reshape(16, depth // 16, width),
                out_weight[0].reshape(16, -1, 2, width)[:, :, 0],
                out_weight[0].reshape(16, -1, 2, width)[:, :, 1],
            ],
            axis=1,
        )
        piece = lax.dynamic_index_in_dim(native, mine, 0, keepdims=False)
        column = lax.all_gather(piece, "dp", axis=0)
        rolled = lax.dynamic_slice_in_dim(jnp.concatenate([column, column], axis=0), chip + 1, bands - 1, 0)
        others = lax.all_gather(rolled, ("y", "core"), axis=0)
        strip = lax.dynamic_index_in_dim(dec_weight.reshape(16, depth // 16, -1), mine, 0, keepdims=False)
        matrix = lax.all_gather(lax.all_gather(strip, "section", axis=0), ("y", "core"), axis=0)

        labels = regions[0, 0]
        labels = jnp.where(parity == core, labels, to_other_core(labels, range(sections)))
        labels = labels.reshape(2, 2, 2, half)
        labels = jnp.where(core == 0, labels, labels[::-1]).transpose(0, 2, 1, 3).reshape(-1)
        lk = labels[None, :]
        lq = labels[:quad * 2, None]

        even = chip % 2 == 0
        tokens = tokens[:, 0, 0]

        def first(flip):
            def route(s, w, d):
                return (s, (w // 2) * 2 + d // 2, chip_of(w % 2, d % 2 ^ flip))
            payload = jnp.where(even if flip == 0 else jnp.logical_not(even), tokens[0], tokens[1])
            return send(payload, route, (0,))

        near, far = first(0), first(1)
        band0 = jnp.where(micro == 0, near, far)
        band1 = jnp.where(micro == 0, far, near)
        own_a = jnp.concatenate([band0[:half], band1[:half]], axis=0)
        own_b = jnp.concatenate([band0[half:], band1[half:]], axis=0)

        def same(s, w, d):
            return (s + 1, w, d)

        def behind(s, w, d):
            window = (w // 2) * 2 + parity_of(d) - 1
            return (s + 1, (window % windows) // 2 * 2 + w % 2, chip_of(window % 2, d >> 1))

        for step in range(sections):
            far_a = to_other_core(own_a, (step,))
            far_b = to_other_core(own_b, (step,))
            out_a, out_b = layer(lq, lk, norm_gain, own_a, own_b, far_a, far_b, native, others)
            if step + 1 < sections:
                own_a = send(out_b, same, (step,))
                own_b = send(out_a, behind, (step,))
        last = sections - 1
        values = decode(final_gain[None, :], out_a, out_b, matrix)

        flipped = micro == 1

        def home(flip, shift):
            def route(s, w, d):
                window = (w // 2) * 2 + parity_of(d) - shift
                return (s, window % windows, 2 * (w % 2) + ((d >> 1) ^ flip))
            low = 0 if shift else quad
            pieces = values[:, low:low + half], values[:, low + half:low + quad]
            swap = flipped if flip == 0 else jnp.logical_not(flipped)
            return send(jnp.where(swap, pieces[1], pieces[0]), route, (last,))

        arrived = [[home(flip, shift) for shift in (0, 1)] for flip in (0, 1)]
        arrived = [jnp.concatenate(pair, axis=1) for pair in arrived]
        first_micro = jnp.where(even, arrived[0], arrived[1])
        second_micro = jnp.where(even, arrived[1], arrived[0])
        result = jnp.stack([first_micro, second_micro], axis=1)
        shown = result[last]
        for target in range(last):
            there = send(result[target], lambda s, w, d: (target, w, d), (last,))
            shown = jnp.where(section == target, there, shown)
        return shown[:, None, None]

    return jax.shard_map(
        body,
        mesh=fine,
        in_specs=(
            P(None, WIN, "dp", None, None),
            P("section", WIN, None),
            P("section", None),
            P("section", None, None, "dp"),
            P("section", "dp", None),
            P(),
            P(None, "section"),
        ),
        out_specs=P(None, WIN, "dp", None, "section"),
        check_vma=False,
    )
```

```python
import jax
import jax.numpy as jnp
import numpy as np
from jax import lax
from jax.experimental import pallas as pl
from jax.experimental.pallas import tpu as pltpu
from jax.sharding import Mesh
from jax.sharding import PartitionSpec as P

HEAD = 64
AXES = ("section", "x", "y", "core", "dp")
WIN = ("x", "y", "core")


def chip_of(parity, micro):
    return 2 * micro + (parity ^ micro)


def parity_of(chip):
    return (chip ^ (chip >> 1)) & 1


def norm(values, gain):
    center = values - jnp.mean(values, axis=-1, keepdims=True)
    spread = jnp.mean(center * center, axis=-1, keepdims=True)
    return (center * lax.rsqrt(spread + 1e-05) * gain).astype(jnp.bfloat16)


def layer_kernel(lq, lk, gain, own_a, own_b, far_a, far_b, native, others, out_a, out_b, normed, acc):
    slices, per, width = native.shape
    inner = width // 3
    heads = inner // HEAD
    rows = per * 3 // 4
    orows = per // 8
    part = own_a.shape[0]
    half = 2 * part
    for index, ref in enumerate((own_a, own_b, far_a, far_b)):
        normed[index * part:(index + 1) * part, :] = norm(ref[...].astype(jnp.float32), gain[...])
    allowed = lq[...] == lk[...]
    head_of = lax.broadcasted_iota(jnp.int32, (half, inner), 1) // HEAD
    for step in range(others.shape[1] + 1):
        def block(low, count):
            value = native[:, low:low + count, :] if step == 0 else others[:, step - 1, low:low + count, :]
            return value.reshape(slices * count, width)

        weight = block(0, rows)
        keyval = jnp.dot(normed[...], weight[:, inner:], preferred_element_type=jnp.float32).astype(jnp.bfloat16)
        query = jnp.dot(normed[:half, :], weight[:, :inner], preferred_element_type=jnp.float32)
        query = (query * (HEAD ** -0.5)).astype(jnp.bfloat16)
        key, value = keyval[:, :inner], keyval[:, inner:]
        stacked = jnp.concatenate(
            [jnp.where(head_of == head, query, jnp.zeros_like(query)) for head in range(heads)], axis=0
        )
        scores = lax.dot_general(stacked, key, (((1,), (1,)), ((), ())), preferred_element_type=jnp.float32)
        scores = jnp.where(jnp.concatenate([allowed] * heads, axis=0), scores, -jnp.inf)
        weights = jnp.exp(scores - jnp.max(scores, axis=-1, keepdims=True))
        total = jnp.sum(weights, axis=-1, keepdims=True)
        mixed = jnp.dot(weights.astype(jnp.bfloat16), value, preferred_element_type=jnp.float32) / total
        blended = mixed[:half]
        for head in range(1, heads):
            blended = jnp.where(head_of == head, mixed[head * half:(head + 1) * half], blended)
        blended = blended.astype(jnp.bfloat16)
        for side in range(2):
            update = jnp.dot(blended, block(rows + side * orows, orows), preferred_element_type=jnp.float32)
            update = update.astype(jnp.bfloat16).astype(jnp.float32)
            cols = slice(side * width, (side + 1) * width)
            if step == 0:
                acc[:, cols] = update
            else:
                acc[:, cols] += update
    out_a[...] = (own_a[...].astype(jnp.float32) + acc[:part, :]).astype(jnp.bfloat16)
    out_b[...] = (own_b[...].astype(jnp.float32) + acc[part:, :]).astype(jnp.bfloat16)


def layer(lq, lk, gain, own_a, own_b, far_a, far_b, native, others):
    part, depth = own_a.shape
    vmem = pl.BlockSpec(memory_space=pltpu.VMEM)
    shape = jax.ShapeDtypeStruct((part, depth), jnp.bfloat16)
    return pl.pallas_call(
        layer_kernel,
        out_shape=(shape, shape),
        in_specs=[vmem] * 9,
        out_specs=(vmem, vmem),
        scratch_shapes=[
            pltpu.VMEM((4 * part, depth), jnp.bfloat16),
            pltpu.VMEM((2 * part, depth), jnp.float32),
        ],
        compiler_params=pltpu.CompilerParams(vmem_limit_bytes=14 << 20),
        cost_estimate=pl.CostEstimate(flops=2_600_000_000, bytes_accessed=14_000_000, transcendentals=524288),
        name="layer",
    )(lq, lk, gain, own_a, own_b, far_a, far_b, native, others)


def decode_kernel(gain, part_a, part_b, matrix, out):
    rows = jnp.concatenate([part_a[...], part_b[...]], axis=0).astype(jnp.float32)
    final = norm(rows, gain[...])
    slices, sections, per, width = matrix.shape
    for section in range(sections):
        weight = matrix[:, section].reshape(slices * per, width)
        out[section] = jnp.dot(final, weight, preferred_element_type=jnp.float32).astype(jnp.bfloat16)


def decode(gain, part_a, part_b, matrix):
    vmem = pl.BlockSpec(memory_space=pltpu.VMEM)
    return pl.pallas_call(
        decode_kernel,
        out_shape=jax.ShapeDtypeStruct((matrix.shape[1], 2 * part_a.shape[0], matrix.shape[3]), jnp.bfloat16),
        in_specs=[vmem] * 4,
        out_specs=vmem,
        compiler_params=pltpu.CompilerParams(vmem_limit_bytes=24 << 20),
        cost_estimate=pl.CostEstimate(flops=450_000_000, bytes_accessed=4_500_000, transcendentals=0),
        name="decode",
    )(gain, part_a, part_b, matrix)


def solution(mesh):
    sections, windows, bands = (mesh.shape[name] for name in ("section", "win", "dp"))
    fine = Mesh(np.asarray(mesh.devices).reshape(sections, windows // 16, 8, 2, bands), AXES)
    chips = windows // 2

    def place(section, window, chip):
        return (section * windows + window % windows) * bands + chip

    def send(value, route, sources):
        pairs = []
        for section in sources:
            for window in range(windows):
                for chip in range(bands):
                    target = route(section, window, chip)
                    if target is not None:
                        pairs.append((place(section, window, chip), place(*target)))
        return lax.ppermute(value, AXES, pairs)

    def to_other_core(value, sources):
        return send(value, lambda s, w, d: (s, w ^ 1, d), sources)

    def body(tokens, regions, norm_gain, qkv_weight, out_weight, final_gain, dec_weight):
        section = lax.axis_index("section")
        core = lax.axis_index("core")
        chip = lax.axis_index("dp")
        mine = lax.axis_index("y") * 2 + core
        depth = tokens.shape[-1]
        quad = tokens.shape[3]
        half = quad // 2
        micro = chip >> 1
        parity = (chip ^ (chip >> 1)) & 1
        width = qkv_weight.shape[2] * qkv_weight.shape[3]

        low = mine * (depth // 16)
        orows = out_weight.shape[1] // 16

        def slab(rows, outs):
            return jnp.concatenate([rows, outs[..., :width], outs[..., width:]], axis=-2)

        piece = slab(
            lax.dynamic_slice_in_dim(qkv_weight[0], low, depth // 16, 0).reshape(-1, width),
            lax.dynamic_slice_in_dim(out_weight[0], mine * orows, orows, 0),
        )
        column = lax.all_gather(piece, "dp", axis=0)
        rolled = lax.dynamic_slice_in_dim(jnp.concatenate([column, column], axis=0), chip + 1, bands - 1, 0)
        others = lax.all_gather(rolled, ("y", "core"), axis=0)
        qkv_weight, out_weight, dec_weight, tokens, regions, _ = lax.optimization_barrier(
            (qkv_weight, out_weight, dec_weight, tokens, regions, rolled)
        )
        native = slab(qkv_weight[0].reshape(16, depth // 16, width), out_weight[0].reshape(16, orows, 2 * width))
        strip = lax.dynamic_slice_in_dim(dec_weight, low, depth // 16, 0)
        matrix = lax.all_gather(lax.all_gather(strip, "section", axis=0), ("y", "core"), axis=0)

        labels = regions[0, 0]
        labels = jnp.where(parity == core, labels, to_other_core(labels, range(sections)))
        labels = labels.reshape(2, 2, 2, half)
        labels = jnp.where(core == 0, labels, labels[::-1]).transpose(0, 2, 1, 3).reshape(-1)
        lk = labels[None, :]
        lq = labels[:quad * 2, None]

        even = chip % 2 == 0
        tokens = tokens[:, 0, 0]

        def first(flip):
            def route(s, w, d):
                return (s, (w // 2) * 2 + d // 2, chip_of(w % 2, d % 2 ^ flip))
            payload = jnp.where(even if flip == 0 else jnp.logical_not(even), tokens[0], tokens[1])
            return send(payload, route, (0,))

        near, far = first(0), first(1)
        band0 = jnp.where(micro == 0, near, far)
        band1 = jnp.where(micro == 0, far, near)
        own_a = jnp.concatenate([band0[:half], band1[:half]], axis=0)
        own_b = jnp.concatenate([band0[half:], band1[half:]], axis=0)

        def same(s, w, d):
            return (s + 1, w, d)

        def behind(s, w, d):
            window = (w // 2) * 2 + parity_of(d) - 1
            return (s + 1, (window % windows) // 2 * 2 + w % 2, chip_of(window % 2, d >> 1))

        for step in range(sections):
            far_a = to_other_core(own_a, (step,))
            far_b = to_other_core(own_b, (step,))
            out_a, out_b = layer(lq, lk, norm_gain, own_a, own_b, far_a, far_b, native, others)
            if step + 1 < sections:
                own_a = send(out_b, same, (step,))
                own_b = send(out_a, behind, (step,))
        last = sections - 1
        values = decode(final_gain[None, :], out_a, out_b, matrix)

        values = values.reshape(sections, 2, 2, half, -1)
        flipped = micro == 1

        def home(flip):
            def route(s, w, d):
                return (s, (w // 2) * 2 + parity_of(d), 2 * (w % 2) + ((d >> 1) ^ flip))
            swap = flipped if flip == 0 else jnp.logical_not(flipped)
            return send(jnp.where(swap, values[:, :, 1], values[:, :, 0]), route, (last,))

        straight, crossed = home(0), home(1)
        result = jnp.stack(
            [jnp.where(even, straight, crossed), jnp.where(even, crossed, straight)], axis=1
        )
        shown = None
        for target in range(sections):
            ahead = send(result[target, :, 0], lambda s, w, d: (target, w - 1, d), (last,))
            kept = result[target, :, 1]
            if target != last:
                kept = send(kept, lambda s, w, d: (target, w, d), (last,))
            here = jnp.concatenate([kept, ahead], axis=1)
            shown = here if shown is None else jnp.where(section == target, here, shown)
        return shown[:, None, None]

    return jax.shard_map(
        body,
        mesh=fine,
        in_specs=(
            P(None, WIN, "dp", None, None),
            P("section", WIN, None),
            P("section", None),
            P("section", None, None, "dp"),
            P("section", "dp", None),
            P(),
            P(None, "section"),
        ),
        out_specs=P(None, WIN, "dp", None, "section"),
        check_vma=False,
    )
```

```python
import jax
import jax.numpy as jnp
import numpy as np
from jax import lax
from jax.experimental import pallas as pl
from jax.experimental.pallas import tpu as pltpu
from jax.sharding import Mesh
from jax.sharding import PartitionSpec as P

HEAD = 64
AXES = ("section", "x", "y", "core", "dp")
WIN = ("x", "y", "core")


def chip_of(parity, micro):
    return 2 * micro + (parity ^ micro)


def parity_of(chip):
    return (chip ^ (chip >> 1)) & 1


def norm(values, gain):
    center = values - jnp.mean(values, axis=-1, keepdims=True)
    spread = jnp.mean(center * center, axis=-1, keepdims=True)
    return (center * lax.rsqrt(spread + 1e-05) * gain).astype(jnp.bfloat16)


def layer_kernel(lq, lk, gain, own_a, own_b, far_a, far_b, native, others, out_a, out_b, normed, acc):
    slices, per, width = native.shape
    inner = width // 3
    heads = inner // HEAD
    rows = per * 3 // 4
    orows = per // 8
    part = own_a.shape[0]
    half = 2 * part
    for index, ref in enumerate((own_a, own_b, far_a, far_b)):
        normed[index * part:(index + 1) * part, :] = norm(ref[...].astype(jnp.float32), gain[...])
    allowed = lq[...] == lk[...]
    head_of = lax.broadcasted_iota(jnp.int32, (half, inner), 1) // HEAD
    for step in range(others.shape[1] + 1):
        def block(low, count):
            value = native[:, low:low + count, :] if step == 0 else others[:, step - 1, low:low + count, :]
            return value.reshape(slices * count, width)

        weight = block(0, rows)
        keyval = jnp.dot(normed[...], weight[:, inner:], preferred_element_type=jnp.float32).astype(jnp.bfloat16)
        query = jnp.dot(normed[:half, :], weight[:, :inner], preferred_element_type=jnp.float32)
        query = (query * (HEAD ** -0.5)).astype(jnp.bfloat16)
        key, value = keyval[:, :inner], keyval[:, inner:]
        stacked = jnp.concatenate(
            [jnp.where(head_of == head, query, jnp.zeros_like(query)) for head in range(heads)], axis=0
        )
        scores = lax.dot_general(stacked, key, (((1,), (1,)), ((), ())), preferred_element_type=jnp.float32)
        scores = jnp.where(jnp.concatenate([allowed] * heads, axis=0), scores, -jnp.inf)
        weights = jnp.exp(scores - jnp.max(scores, axis=-1, keepdims=True))
        total = jnp.sum(weights, axis=-1, keepdims=True)
        mixed = jnp.dot(weights.astype(jnp.bfloat16), value, preferred_element_type=jnp.float32) / total
        blended = mixed[:half]
        for head in range(1, heads):
            blended = jnp.where(head_of == head, mixed[head * half:(head + 1) * half], blended)
        blended = blended.astype(jnp.bfloat16)
        for side in range(2):
            update = jnp.dot(blended, block(rows + side * orows, orows), preferred_element_type=jnp.float32)
            update = update.astype(jnp.bfloat16).astype(jnp.float32)
            cols = slice(side * width, (side + 1) * width)
            if step == 0:
                acc[:, cols] = update
            else:
                acc[:, cols] += update
    out_a[...] = (own_a[...].astype(jnp.float32) + acc[:part, :]).astype(jnp.bfloat16)
    out_b[...] = (own_b[...].astype(jnp.float32) + acc[part:, :]).astype(jnp.bfloat16)


def layer(lq, lk, gain, own_a, own_b, far_a, far_b, native, others):
    part, depth = own_a.shape
    vmem = pl.BlockSpec(memory_space=pltpu.VMEM)
    shape = jax.ShapeDtypeStruct((part, depth), jnp.bfloat16)
    return pl.pallas_call(
        layer_kernel,
        out_shape=(shape, shape),
        in_specs=[vmem] * 9,
        out_specs=(vmem, vmem),
        scratch_shapes=[
            pltpu.VMEM((4 * part, depth), jnp.bfloat16),
            pltpu.VMEM((2 * part, depth), jnp.float32),
        ],
        compiler_params=pltpu.CompilerParams(vmem_limit_bytes=14 << 20),
        cost_estimate=pl.CostEstimate(flops=2_600_000_000, bytes_accessed=14_000_000, transcendentals=524288),
        name="layer",
    )(lq, lk, gain, own_a, own_b, far_a, far_b, native, others)


def decode_kernel(gain, part_a, part_b, matrix, out):
    rows = jnp.concatenate([part_a[...], part_b[...]], axis=0).astype(jnp.float32)
    final = norm(rows, gain[...])
    slices, sections, per, width = matrix.shape
    for section in range(sections):
        weight = matrix[:, section].reshape(slices * per, width)
        out[section] = jnp.dot(final, weight, preferred_element_type=jnp.float32).astype(jnp.bfloat16)


def decode(gain, part_a, part_b, matrix):
    vmem = pl.BlockSpec(memory_space=pltpu.VMEM)
    return pl.pallas_call(
        decode_kernel,
        out_shape=jax.ShapeDtypeStruct((matrix.shape[1], 2 * part_a.shape[0], matrix.shape[3]), jnp.bfloat16),
        in_specs=[vmem] * 4,
        out_specs=vmem,
        compiler_params=pltpu.CompilerParams(vmem_limit_bytes=24 << 20),
        cost_estimate=pl.CostEstimate(flops=450_000_000, bytes_accessed=4_500_000, transcendentals=0),
        name="decode",
    )(gain, part_a, part_b, matrix)


def solution(mesh):
    sections, windows, bands = (mesh.shape[name] for name in ("section", "win", "dp"))
    fine = Mesh(np.asarray(mesh.devices).reshape(sections, windows // 16, 8, 2, bands), AXES)
    chips = windows // 2

    def place(section, window, chip):
        return (section * windows + window % windows) * bands + chip

    def send(value, route, sources):
        pairs = []
        for section in sources:
            for window in range(windows):
                for chip in range(bands):
                    target = route(section, window, chip)
                    if target is not None:
                        pairs.append((place(section, window, chip), place(*target)))
        return lax.ppermute(value, AXES, pairs)

    def to_other_core(value, sources):
        return send(value, lambda s, w, d: (s, w ^ 1, d), sources)

    def body(tokens, regions, norm_gain, qkv_weight, out_weight, final_gain, dec_weight):
        section = lax.axis_index("section")
        core = lax.axis_index("core")
        chip = lax.axis_index("dp")
        mine = lax.axis_index("y") * 2 + core
        depth = tokens.shape[-1]
        quad = tokens.shape[3]
        half = quad // 2
        micro = chip >> 1
        parity = (chip ^ (chip >> 1)) & 1
        width = qkv_weight.shape[2] * qkv_weight.shape[3]

        low = mine * (depth // 16)
        orows = out_weight.shape[1] // 16

        def slab(rows, outs):
            return jnp.concatenate([rows, outs[..., :width], outs[..., width:]], axis=-2)

        piece = slab(
            lax.dynamic_slice_in_dim(qkv_weight[0], low, depth // 16, 0).reshape(-1, width),
            lax.dynamic_slice_in_dim(out_weight[0], mine * orows, orows, 0),
        )

        def upward(value, sources):
            routes = [
                (lambda s, w, d, turn=turn: (s, w, (d - turn) % bands)) for turn in (bands - 1, 1, *range(2, bands - 1))
            ]
            got = [send(value, route, sources) for route in routes]
            return jnp.stack([got[1], *got[2:], got[0]])

        later = tuple(range(1, sections))
        lead = upward(piece, (0,))
        mark = lead[-1, :16, :128] + lead[0, :16, :128] + lead[1, :16, :128]
        heard = jnp.zeros_like(mark)
        for target in later:
            heard += send(mark, lambda s, w, d: (target, w, d), (0,))
        piece = jnp.where(heard[:1, :1] > 1e30, jnp.zeros_like(piece), piece)
        rolled = jnp.where(section == 0, lead, upward(piece, later))
        others = lax.all_gather(rolled, ("y", "core"), axis=0)
        qkv_weight, out_weight, dec_weight, tokens, regions, _ = lax.optimization_barrier(
            (qkv_weight, out_weight, dec_weight, tokens, regions, rolled)
        )
        native = slab(qkv_weight[0].reshape(16, depth // 16, width), out_weight[0].reshape(16, orows, 2 * width))

        labels = regions[0, 0]
        labels = jnp.where(parity == core, labels, to_other_core(labels, range(sections)))
        labels = labels.reshape(2, 2, 2, half)
        labels = jnp.where(core == 0, labels, labels[::-1]).transpose(0, 2, 1, 3).reshape(-1)
        lk = labels[None, :]
        lq = labels[:quad * 2, None]

        even = chip % 2 == 0
        tokens = tokens[:, 0, 0]

        def first(flip):
            def route(s, w, d):
                return (s, (w // 2) * 2 + d // 2, chip_of(w % 2, d % 2 ^ flip))
            payload = jnp.where(even if flip == 0 else jnp.logical_not(even), tokens[0], tokens[1])
            return send(payload, route, (0,))

        near, far = first(0), first(1)
        band0 = jnp.where(micro == 0, near, far)
        band1 = jnp.where(micro == 0, far, near)
        own_a = jnp.concatenate([band0[:half], band1[:half]], axis=0)
        own_b = jnp.concatenate([band0[half:], band1[half:]], axis=0)

        dec_weight, own_a, own_b = lax.optimization_barrier((dec_weight, own_a, own_b))
        strip = lax.dynamic_slice_in_dim(dec_weight, low, depth // 16, 0)
        matrix = lax.all_gather(lax.all_gather(strip, "section", axis=0), ("y", "core"), axis=0)

        def same(s, w, d):
            return (s + 1, w, d)

        def behind(s, w, d):
            window = (w // 2) * 2 + parity_of(d) - 1
            return (s + 1, (window % windows) // 2 * 2 + w % 2, chip_of(window % 2, d >> 1))

        for step in range(sections):
            far_a = to_other_core(own_a, (step,))
            far_b = to_other_core(own_b, (step,))
            out_a, out_b = layer(lq, lk, norm_gain, own_a, own_b, far_a, far_b, native, others)
            if step + 1 < sections:
                own_a = send(out_b, same, (step,))
                own_b = send(out_a, behind, (step,))
        last = sections - 1
        values = decode(final_gain[None, :], out_a, out_b, matrix)

        values = values.reshape(sections, 2, 2, half, -1)
        flipped = micro == 1

        def home(flip):
            def route(s, w, d):
                return (s, (w // 2) * 2 + parity_of(d), 2 * (w % 2) + ((d >> 1) ^ flip))
            swap = flipped if flip == 0 else jnp.logical_not(flipped)
            return send(jnp.where(swap, values[:, :, 1], values[:, :, 0]), route, (last,))

        straight, crossed = home(0), home(1)
        result = jnp.stack(
            [jnp.where(even, straight, crossed), jnp.where(even, crossed, straight)], axis=1
        )
        shown = None
        for target in range(sections):
            ahead = send(result[target, :, 0], lambda s, w, d: (target, w - 1, d), (last,))
            kept = result[target, :, 1]
            if target != last:
                kept = send(kept, lambda s, w, d: (target, w, d), (last,))
            here = jnp.concatenate([kept, ahead], axis=1)
            shown = here if shown is None else jnp.where(section == target, here, shown)
        return shown[:, None, None]

    return jax.shard_map(
        body,
        mesh=fine,
        in_specs=(
            P(None, WIN, "dp", None, None),
            P("section", WIN, None),
            P("section", None),
            P("section", None, None, "dp"),
            P("section", "dp", None),
            P(),
            P(None, "section"),
        ),
        out_specs=P(None, WIN, "dp", None, "section"),
        check_vma=False,
    )
```

```python
import functools

import jax
import jax.numpy as jnp
import numpy as np
from jax import lax
from jax.experimental import pallas as pl
from jax.experimental.pallas import tpu as pltpu
from jax.sharding import Mesh
from jax.sharding import PartitionSpec as P

HEAD = 64
AXES = ("section", "x", "y", "core", "dp")
WIN = ("x", "y", "core")


def chip_of(parity, micro):
    return 2 * micro + (parity ^ micro)


def parity_of(chip):
    return (chip ^ (chip >> 1)) & 1


def norm(values, gain):
    center = values - jnp.mean(values, axis=-1, keepdims=True)
    spread = jnp.mean(center * center, axis=-1, keepdims=True)
    return (center * lax.rsqrt(spread + 1e-05) * gain).astype(jnp.bfloat16)


def layer_kernel(lq, lk, gain, own_a, own_b, far_a, far_b, native, others, out_a, out_b, normed, acc):
    slices, per, width = native.shape
    inner = width // 3
    heads = inner // HEAD
    rows = per * 3 // 4
    orows = per // 8
    part = own_a.shape[0]
    half = 2 * part
    for index, ref in enumerate((own_a, own_b, far_a, far_b)):
        normed[index * part:(index + 1) * part, :] = norm(ref[...].astype(jnp.float32), gain[...])
    allowed = lq[...] == lk[...]
    head_of = lax.broadcasted_iota(jnp.int32, (half, inner), 1) // HEAD
    for step in range(others.shape[1] + 1):
        def block(low, count):
            value = native[:, low:low + count, :] if step == 0 else others[:, step - 1, low:low + count, :]
            return value.reshape(slices * count, width)

        weight = block(0, rows)
        keyval = jnp.dot(normed[...], weight[:, inner:], preferred_element_type=jnp.float32).astype(jnp.bfloat16)
        query = jnp.dot(normed[:half, :], weight[:, :inner], preferred_element_type=jnp.float32)
        query = (query * (HEAD ** -0.5)).astype(jnp.bfloat16)
        key, value = keyval[:, :inner], keyval[:, inner:]
        stacked = jnp.concatenate(
            [jnp.where(head_of == head, query, jnp.zeros_like(query)) for head in range(heads)], axis=0
        )
        scores = lax.dot_general(stacked, key, (((1,), (1,)), ((), ())), preferred_element_type=jnp.float32)
        scores = jnp.where(jnp.concatenate([allowed] * heads, axis=0), scores, -jnp.inf)
        weights = jnp.exp(scores - jnp.max(scores, axis=-1, keepdims=True))
        total = jnp.sum(weights, axis=-1, keepdims=True)
        mixed = jnp.dot(weights.astype(jnp.bfloat16), value, preferred_element_type=jnp.float32) / total
        blended = mixed[:half]
        for head in range(1, heads):
            blended = jnp.where(head_of == head, mixed[head * half:(head + 1) * half], blended)
        blended = blended.astype(jnp.bfloat16)
        for side in range(2):
            update = jnp.dot(blended, block(rows + side * orows, orows), preferred_element_type=jnp.float32)
            update = update.astype(jnp.bfloat16).astype(jnp.float32)
            cols = slice(side * width, (side + 1) * width)
            if step == 0:
                acc[:, cols] = update
            else:
                acc[:, cols] += update
    out_a[...] = (own_a[...].astype(jnp.float32) + acc[:part, :]).astype(jnp.bfloat16)
    out_b[...] = (own_b[...].astype(jnp.float32) + acc[part:, :]).astype(jnp.bfloat16)


def layer(lq, lk, gain, own_a, own_b, far_a, far_b, native, others):
    part, depth = own_a.shape
    vmem = pl.BlockSpec(memory_space=pltpu.VMEM)
    shape = jax.ShapeDtypeStruct((part, depth), jnp.bfloat16)
    return pl.pallas_call(
        layer_kernel,
        out_shape=(shape, shape),
        in_specs=[vmem] * 9,
        out_specs=(vmem, vmem),
        scratch_shapes=[
            pltpu.VMEM((4 * part, depth), jnp.bfloat16),
            pltpu.VMEM((2 * part, depth), jnp.float32),
        ],
        compiler_params=pltpu.CompilerParams(vmem_limit_bytes=14 << 20),
        cost_estimate=pl.CostEstimate(flops=2_600_000_000, bytes_accessed=14_000_000, transcendentals=524288),
        name="layer",
    )(lq, lk, gain, own_a, own_b, far_a, far_b, native, others)


def decode_kernel(gain, part_a, part_b, matrix, out):
    rows = jnp.concatenate([part_a[...], part_b[...]], axis=0).astype(jnp.float32)
    final = norm(rows, gain[...])
    for section in range(matrix.shape[0]):
        out[section] = lax.dot_general(
            final, matrix[section], (((1,), (1,)), ((), ())), preferred_element_type=jnp.float32
        ).astype(jnp.bfloat16)


def decode(gain, part_a, part_b, matrix):
    vmem = pl.BlockSpec(memory_space=pltpu.VMEM)
    return pl.pallas_call(
        decode_kernel,
        out_shape=jax.ShapeDtypeStruct((matrix.shape[0], 2 * part_a.shape[0], matrix.shape[1]), jnp.bfloat16),
        in_specs=[vmem] * 4,
        out_specs=vmem,
        compiler_params=pltpu.CompilerParams(vmem_limit_bytes=24 << 20),
        cost_estimate=pl.CostEstimate(flops=450_000_000, bytes_accessed=4_500_000, transcendentals=0),
        name="decode",
    )(gain, part_a, part_b, matrix)


def gather_kernel(near_keys, far_keys, place, near, far, near_other, far_other, out, sems):
    chunk = near.shape[2]
    row, core = place[0], place[1]
    copies = []
    for keys, source, side in (
        (near_keys, near, core), (near_keys, near_other, 1 - core), (far_keys, far, core), (far_keys, far_other, 1 - core)
    ):
        for index, (which, at) in enumerate(keys):
            target = lax.rem(row + (at + 8), 8) * 2 + side
            copies.append(
                pltpu.make_async_copy(
                    source.at[index], out.at[target, :, which * chunk:(which + 1) * chunk, :], sems.at[len(copies)]
                )
            )
    for copy in copies:
        copy.start()
    for copy in copies:
        copy.wait()


def gather_blocks(near_keys, far_keys, place, *blocks):
    _, turns, chunk, width = blocks[0].shape
    hbm = pl.BlockSpec(memory_space=pl.ANY)
    return pl.pallas_call(
        functools.partial(gather_kernel, near_keys, far_keys),
        out_shape=jax.ShapeDtypeStruct((16, turns, 2 * chunk, width), jnp.bfloat16),
        in_specs=[pl.BlockSpec(memory_space=pltpu.SMEM)] + [hbm] * 4,
        out_specs=pl.BlockSpec(memory_space=pltpu.VMEM),
        scratch_shapes=[pltpu.SemaphoreType.DMA((2 * (len(near_keys) + len(far_keys)),))],
        compiler_params=pltpu.CompilerParams(vmem_limit_bytes=14 << 20),
        cost_estimate=pl.CostEstimate(flops=0, bytes_accessed=20_000_000, transcendentals=0),
        name="gather_blocks",
    )(place, *blocks)


def solution(mesh):
    sections, windows, bands = (mesh.shape[name] for name in ("section", "win", "dp"))
    fine = Mesh(np.asarray(mesh.devices).reshape(sections, windows // 16, 8, 2, bands), AXES)
    chips = windows // 2

    def place(section, window, chip):
        return (section * windows + window % windows) * bands + chip

    def send(value, route, sources):
        pairs = []
        for section in sources:
            for window in range(windows):
                for chip in range(bands):
                    target = route(section, window, chip)
                    if target is not None:
                        pairs.append((place(section, window, chip), place(*target)))
        return lax.ppermute(value, AXES, pairs)

    def to_other_core(value, sources):
        return send(value, lambda s, w, d: (s, w ^ 1, d), sources)

    def body(tokens, regions, norm_gain, qkv_weight, out_weight, final_gain, dec_weight):
        section = lax.axis_index("section")
        core = lax.axis_index("core")
        chip = lax.axis_index("dp")
        mine = lax.axis_index("y") * 2 + core
        depth = tokens.shape[-1]
        quad = tokens.shape[3]
        half = quad // 2
        micro = chip >> 1
        parity = (chip ^ (chip >> 1)) & 1
        width = qkv_weight.shape[2] * qkv_weight.shape[3]

        low = mine * (depth // 16)
        orows = out_weight.shape[1] // 16

        def slab(rows, outs):
            return jnp.concatenate([rows, outs[..., :width], outs[..., width:]], axis=-2)

        across = windows // 16
        piece = slab(
            lax.dynamic_slice_in_dim(qkv_weight[0], low, depth // 16, 0).reshape(-1, width),
            lax.dynamic_slice_in_dim(out_weight[0], mine * orows, orows, 0),
        )
        share = piece.shape[0] // across
        piece = lax.dynamic_slice_in_dim(piece, lax.axis_index("x") * share, share, 0)
        column = lax.all_to_all(jnp.broadcast_to(piece, (bands,) + piece.shape), "dp", 0, 0)
        rolled = lax.dynamic_slice_in_dim(jnp.concatenate([column, column], axis=0), chip + 1, bands - 1, 0)
        block = lax.all_to_all(jnp.broadcast_to(rolled, (across,) + rolled.shape), "x", 0, 0)
        block = block.transpose(1, 0, 2, 3).reshape(bands - 1, across * share, width)
        everywhere = range(sections)

        def along(value, turn):
            def route(s, w, d):
                return (s, w // 16 * 16 + (w % 16 // 2 + turn) % 8 * 2 + w % 2, d)
            return send(value, route, everywhere)

        chunk = block.shape[1] // 2
        near_blocks, far_blocks = [], []
        held = [{0: block[:, :chunk]}, {0: block[:, chunk:]}]
        for hop in range(1, 5):
            for turn in (1, -1):
                for which in range(2):
                    if hop < 4 or (which == 0) == (turn == 1):
                        held[which][-turn * hop] = along(held[which][-turn * (hop - 1)], turn)
        near_keys = [(which, at) for which in range(2) for at in held[which] if abs(at) <= 2]
        far_keys = [(which, at) for which in range(2) for at in held[which] if abs(at) > 2]
        near_blocks = jnp.stack([held[which][at] for which, at in near_keys])
        far_blocks = jnp.stack([held[which][at] for which, at in far_keys])
        others = gather_blocks(
            near_keys, far_keys, jnp.stack([lax.axis_index("y"), core]).astype(jnp.int32),
            near_blocks, far_blocks, to_other_core(near_blocks, everywhere), to_other_core(far_blocks, everywhere),
        )
        qkv_weight, out_weight, dec_weight, tokens, regions, rolled = lax.optimization_barrier(
            (qkv_weight, out_weight, dec_weight, tokens, regions, rolled)
        )
        native = slab(qkv_weight[0].reshape(16, depth // 16, width), out_weight[0].reshape(16, orows, 2 * width))
        last = sections - 1
        turned = dec_weight.T
        wide = turned.shape[0]
        strip = lax.dynamic_slice_in_dim(turned, core * (wide // 2), wide // 2, 0)
        strips = jnp.stack(
            [send(strip, lambda s, w, d: (last, w, d), (source,)) for source in range(last)]
        )
        matched = to_other_core(strips, (last,))
        strips = jnp.stack([jnp.where(core == 0, strips, matched), jnp.where(core == 0, matched, strips)], axis=1)
        matrix = jnp.concatenate([strips.reshape(last, wide, depth), turned[None]], axis=0)

        labels = regions[0, 0]
        labels = jnp.where(parity == core, labels, to_other_core(labels, range(sections)))
        labels = labels.reshape(2, 2, 2, half)
        labels = jnp.where(core == 0, labels, labels[::-1]).transpose(0, 2, 1, 3).reshape(-1)
        lk = labels[None, :]
        lq = labels[:quad * 2, None]

        even = chip % 2 == 0
        tokens = tokens[:, 0, 0]

        def first(flip):
            def route(s, w, d):
                return (s, (w // 2) * 2 + d // 2, chip_of(w % 2, d % 2 ^ flip))
            payload = jnp.where(even if flip == 0 else jnp.logical_not(even), tokens[0], tokens[1])
            return send(payload, route, (0,))

        near, far = first(0), first(1)
        band0 = jnp.where(micro == 0, near, far)
        band1 = jnp.where(micro == 0, far, near)
        own_a = jnp.concatenate([band0[:half], band1[:half]], axis=0)
        own_b = jnp.concatenate([band0[half:], band1[half:]], axis=0)

        def same(s, w, d):
            return (s + 1, w, d)

        def behind(s, w, d):
            window = (w // 2) * 2 + parity_of(d) - 1
            return (s + 1, (window % windows) // 2 * 2 + w % 2, chip_of(window % 2, d >> 1))

        for step in range(sections):
            far_a = to_other_core(own_a, (step,))
            far_b = to_other_core(own_b, (step,))
            out_a, out_b = layer(lq, lk, norm_gain, own_a, own_b, far_a, far_b, native, others)
            if step + 1 < sections:
                own_a = send(out_b, same, (step,))
                own_b = send(out_a, behind, (step,))
        values = decode(final_gain[None, :], out_a, out_b, matrix)

        values = values.reshape(sections, 2, 2, half, -1)
        flipped = micro == 1

        def home(flip):
            def route(s, w, d):
                return (s, (w // 2) * 2 + parity_of(d), 2 * (w % 2) + ((d >> 1) ^ flip))
            swap = flipped if flip == 0 else jnp.logical_not(flipped)
            return send(jnp.where(swap, values[:, :, 1], values[:, :, 0]), route, (last,))

        straight, crossed = home(0), home(1)
        result = jnp.stack(
            [jnp.where(even, straight, crossed), jnp.where(even, crossed, straight)], axis=1
        )
        shown = None
        for target in range(sections):
            ahead = send(result[target, :, 0], lambda s, w, d: (target, w - 1, d), (last,))
            kept = result[target, :, 1]
            if target != last:
                kept = send(kept, lambda s, w, d: (target, w, d), (last,))
            here = jnp.concatenate([kept, ahead], axis=1)
            shown = here if shown is None else jnp.where(section == target, here, shown)
        return shown[:, None, None]

    return jax.shard_map(
        body,
        mesh=fine,
        in_specs=(
            P(None, WIN, "dp", None, None),
            P("section", WIN, None),
            P("section", None),
            P("section", None, None, "dp"),
            P("section", "dp", None),
            P(),
            P(None, "section"),
        ),
        out_specs=P(None, WIN, "dp", None, "section"),
        check_vma=False,
    )
```

```python
import jax
import jax.numpy as jnp
import numpy as np
from jax import lax
from jax.experimental import pallas as pl
from jax.experimental.pallas import tpu as pltpu
from jax.sharding import Mesh
from jax.sharding import PartitionSpec as P

HEAD = 64
AXES = ("section", "x", "y", "core", "dp")
WIN = ("x", "y", "core")


def chip_of(parity, micro):
    return 2 * micro + (parity ^ micro)


def parity_of(chip):
    return (chip ^ (chip >> 1)) & 1


def norm(values, gain):
    center = values - jnp.mean(values, axis=-1, keepdims=True)
    spread = jnp.mean(center * center, axis=-1, keepdims=True)
    return (center * lax.rsqrt(spread + 1e-05) * gain).astype(jnp.bfloat16)


def layer_kernel(lq, lk, gain, own_a, own_b, far_a, far_b, native, others, out_a, out_b, held, normed, acc, sems):
    quarters, slices, per, width = held.shape
    inner = width // 3
    heads = inner // HEAD
    rows = per * 3 // 4
    orows = per // 8
    part = own_a.shape[0]
    half = 2 * part
    copies = []
    for step in range(quarters):
        source = native if step == 0 else others.at[:, step - 1]
        copies.append(pltpu.make_async_copy(source, held.at[step], sems.at[step]))
        copies[-1].start()
    for index, ref in enumerate((own_a, own_b, far_a, far_b)):
        normed[index * part:(index + 1) * part, :] = norm(ref[...].astype(jnp.float32), gain[...])
    allowed = lq[...] == lk[...]
    head_of = lax.broadcasted_iota(jnp.int32, (half, inner), 1) // HEAD
    for step in range(quarters):
        copies[step].wait()

        def block(low, count):
            return held[step, :, low:low + count, :].reshape(slices * count, width)

        weight = block(0, rows)
        keyval = jnp.dot(normed[...], weight[:, inner:], preferred_element_type=jnp.float32).astype(jnp.bfloat16)
        query = jnp.dot(normed[:half, :], weight[:, :inner], preferred_element_type=jnp.float32)
        query = (query * (HEAD ** -0.5)).astype(jnp.bfloat16)
        key, value = keyval[:, :inner], keyval[:, inner:]
        stacked = jnp.concatenate(
            [jnp.where(head_of == head, query, jnp.zeros_like(query)) for head in range(heads)], axis=0
        )
        scores = lax.dot_general(stacked, key, (((1,), (1,)), ((), ())), preferred_element_type=jnp.float32)
        scores = jnp.where(jnp.concatenate([allowed] * heads, axis=0), scores, -jnp.inf)
        weights = jnp.exp(scores - jnp.max(scores, axis=-1, keepdims=True))
        total = jnp.sum(weights, axis=-1, keepdims=True)
        mixed = jnp.dot(weights.astype(jnp.bfloat16), value, preferred_element_type=jnp.float32) / total
        blended = mixed[:half]
        for head in range(1, heads):
            blended = jnp.where(head_of == head, mixed[head * half:(head + 1) * half], blended)
        blended = blended.astype(jnp.bfloat16)
        for side in range(2):
            update = jnp.dot(blended, block(rows + side * orows, orows), preferred_element_type=jnp.float32)
            update = update.astype(jnp.bfloat16).astype(jnp.float32)
            cols = slice(side * width, (side + 1) * width)
            if step == 0:
                acc[:, cols] = update
            else:
                acc[:, cols] += update
    out_a[...] = (own_a[...].astype(jnp.float32) + acc[:part, :]).astype(jnp.bfloat16)
    out_b[...] = (own_b[...].astype(jnp.float32) + acc[part:, :]).astype(jnp.bfloat16)


def layer(lq, lk, gain, own_a, own_b, far_a, far_b, native, others):
    part, depth = own_a.shape
    quarters = others.shape[1] + 1
    vmem = pl.BlockSpec(memory_space=pltpu.VMEM)
    hbm = pl.BlockSpec(memory_space=pl.ANY)
    shape = jax.ShapeDtypeStruct((part, depth), jnp.bfloat16)
    return pl.pallas_call(
        layer_kernel,
        out_shape=(shape, shape),
        in_specs=[vmem] * 7 + [hbm] * 2,
        out_specs=(vmem, vmem),
        scratch_shapes=[
            pltpu.VMEM((quarters,) + native.shape, jnp.bfloat16),
            pltpu.VMEM((4 * part, depth), jnp.bfloat16),
            pltpu.VMEM((2 * part, depth), jnp.float32),
            pltpu.SemaphoreType.DMA((quarters,)),
        ],
        compiler_params=pltpu.CompilerParams(vmem_limit_bytes=48 << 20),
        cost_estimate=pl.CostEstimate(flops=2_600_000_000, bytes_accessed=14_000_000, transcendentals=524288),
        name="layer",
    )(lq, lk, gain, own_a, own_b, far_a, far_b, native, others)


def decode_kernel(gain, part_a, part_b, matrix, out):
    rows = jnp.concatenate([part_a[...], part_b[...]], axis=0).astype(jnp.float32)
    final = norm(rows, gain[...])
    for section in range(matrix.shape[0]):
        out[section] = lax.dot_general(
            final, matrix[section], (((1,), (1,)), ((), ())), preferred_element_type=jnp.float32
        ).astype(jnp.bfloat16)


def decode(gain, part_a, part_b, matrix):
    vmem = pl.BlockSpec(memory_space=pltpu.VMEM)
    return pl.pallas_call(
        decode_kernel,
        out_shape=jax.ShapeDtypeStruct((matrix.shape[0], 2 * part_a.shape[0], matrix.shape[1]), jnp.bfloat16),
        in_specs=[vmem] * 4,
        out_specs=vmem,
        compiler_params=pltpu.CompilerParams(vmem_limit_bytes=24 << 20),
        cost_estimate=pl.CostEstimate(flops=450_000_000, bytes_accessed=4_500_000, transcendentals=0),
        name="decode",
    )(gain, part_a, part_b, matrix)


def solution(mesh):
    sections, windows, bands = (mesh.shape[name] for name in ("section", "win", "dp"))
    fine = Mesh(np.asarray(mesh.devices).reshape(sections, windows // 16, 8, 2, bands), AXES)
    chips = windows // 2

    def place(section, window, chip):
        return (section * windows + window % windows) * bands + chip

    def send(value, route, sources):
        pairs = []
        for section in sources:
            for window in range(windows):
                for chip in range(bands):
                    target = route(section, window, chip)
                    if target is not None:
                        pairs.append((place(section, window, chip), place(*target)))
        return lax.ppermute(value, AXES, pairs)

    def to_other_core(value, sources):
        return send(value, lambda s, w, d: (s, w ^ 1, d), sources)

    def body(tokens, regions, norm_gain, qkv_weight, out_weight, final_gain, dec_weight):
        section = lax.axis_index("section")
        core = lax.axis_index("core")
        chip = lax.axis_index("dp")
        mine = lax.axis_index("y") * 2 + core
        depth = tokens.shape[-1]
        quad = tokens.shape[3]
        half = quad // 2
        micro = chip >> 1
        parity = (chip ^ (chip >> 1)) & 1
        width = qkv_weight.shape[2] * qkv_weight.shape[3]

        low = mine * (depth // 16)
        orows = out_weight.shape[1] // 16

        def slab(rows, outs):
            return jnp.concatenate([rows, outs[..., :width], outs[..., width:]], axis=-2)

        piece = slab(
            lax.dynamic_slice_in_dim(qkv_weight[0], low, depth // 16, 0).reshape(-1, width),
            lax.dynamic_slice_in_dim(out_weight[0], mine * orows, orows, 0),
        )
        column = lax.all_gather(piece, "dp", axis=0)
        rolled = lax.dynamic_slice_in_dim(jnp.concatenate([column, column], axis=0), chip + 1, bands - 1, 0)
        others = lax.all_gather(rolled, ("y", "core"), axis=0)
        qkv_weight, out_weight, dec_weight, tokens, regions, _ = lax.optimization_barrier(
            (qkv_weight, out_weight, dec_weight, tokens, regions, rolled)
        )
        native = slab(qkv_weight[0].reshape(16, depth // 16, width), out_weight[0].reshape(16, orows, 2 * width))
        last = sections - 1
        turned = dec_weight.T
        wide = turned.shape[0]
        strip = lax.dynamic_slice_in_dim(turned, core * (wide // 2), wide // 2, 0)
        strips = jnp.stack(
            [send(strip, lambda s, w, d: (last, w, d), (source,)) for source in range(last)]
        )
        matched = to_other_core(strips, (last,))
        strips = jnp.stack([jnp.where(core == 0, strips, matched), jnp.where(core == 0, matched, strips)], axis=1)
        matrix = jnp.concatenate([strips.reshape(last, wide, depth), turned[None]], axis=0)

        labels = regions[0, 0]
        labels = jnp.where(parity == core, labels, to_other_core(labels, range(sections)))
        labels = labels.reshape(2, 2, 2, half)
        labels = jnp.where(core == 0, labels, labels[::-1]).transpose(0, 2, 1, 3).reshape(-1)
        lk = labels[None, :]
        lq = labels[:quad * 2, None]

        even = chip % 2 == 0
        tokens = tokens[:, 0, 0]

        def first(flip):
            def route(s, w, d):
                return (s, (w // 2) * 2 + d // 2, chip_of(w % 2, d % 2 ^ flip))
            payload = jnp.where(even if flip == 0 else jnp.logical_not(even), tokens[0], tokens[1])
            return send(payload, route, (0,))

        near, far = first(0), first(1)
        band0 = jnp.where(micro == 0, near, far)
        band1 = jnp.where(micro == 0, far, near)
        own_a = jnp.concatenate([band0[:half], band1[:half]], axis=0)
        own_b = jnp.concatenate([band0[half:], band1[half:]], axis=0)

        def same(s, w, d):
            return (s + 1, w, d)

        def behind(s, w, d):
            window = (w // 2) * 2 + parity_of(d) - 1
            return (s + 1, (window % windows) // 2 * 2 + w % 2, chip_of(window % 2, d >> 1))

        for step in range(sections):
            far_a = to_other_core(own_a, (step,))
            far_b = to_other_core(own_b, (step,))
            out_a, out_b = layer(lq, lk, norm_gain, own_a, own_b, far_a, far_b, native, others)
            if step + 1 < sections:
                own_b = send(out_a, behind, (step,))
                own_a = send(out_b, same, (step,))
        values = decode(final_gain[None, :], out_a, out_b, matrix)

        values = values.reshape(sections, 2, 2, half, -1)
        flipped = micro == 1

        def home(flip):
            def route(s, w, d):
                return (s, (w // 2) * 2 + parity_of(d), 2 * (w % 2) + ((d >> 1) ^ flip))
            swap = flipped if flip == 0 else jnp.logical_not(flipped)
            return send(jnp.where(swap, values[:, :, 1], values[:, :, 0]), route, (last,))

        straight, crossed = home(0), home(1)
        result = jnp.stack(
            [jnp.where(even, straight, crossed), jnp.where(even, crossed, straight)], axis=1
        )
        shown = None
        for target in range(sections):
            ahead = send(result[target, :, 0], lambda s, w, d: (target, w - 1, d), (last,))
            kept = result[target, :, 1]
            if target != last:
                kept = send(kept, lambda s, w, d: (target, w, d), (last,))
            here = jnp.concatenate([kept, ahead], axis=1)
            shown = here if shown is None else jnp.where(section == target, here, shown)
        return shown[:, None, None]

    return jax.shard_map(
        body,
        mesh=fine,
        in_specs=(
            P(None, WIN, "dp", None, None),
            P("section", WIN, None),
            P("section", None),
            P("section", None, None, "dp"),
            P("section", "dp", None),
            P(),
            P(None, "section"),
        ),
        out_specs=P(None, WIN, "dp", None, "section"),
        check_vma=False,
    )
```

```python
import jax
import jax.numpy as jnp
import numpy as np
from jax import lax
from jax.experimental import pallas as pl
from jax.experimental.pallas import tpu as pltpu
from jax.sharding import Mesh
from jax.sharding import PartitionSpec as P

HEAD = 64
AXES = ("section", "x", "y", "core", "dp")
WIN = ("x", "y", "core")


def chip_of(parity, micro):
    return 2 * micro + (parity ^ micro)


def parity_of(chip):
    return (chip ^ (chip >> 1)) & 1


def norm(values, gain):
    center = values - jnp.mean(values, axis=-1, keepdims=True)
    spread = jnp.mean(center * center, axis=-1, keepdims=True)
    return (center * lax.rsqrt(spread + 1e-05) * gain).astype(jnp.bfloat16)


def layer_kernel(lq, lk, gain, own_b, own_a, far_b, far_a, native, others, out_a, out_b, held, normed, acc, sems):
    quarters, slices, per, width = held.shape
    inner = width // 3
    heads = inner // HEAD
    rows = per * 3 // 4
    orows = per // 8
    part = own_a.shape[0]
    half = 2 * part
    copies = []
    for step in range(quarters):
        source = native if step == 0 else others.at[:, step - 1]
        copies.append(pltpu.make_async_copy(source, held.at[step], sems.at[step]))
        copies[-1].start()
    for index, ref in enumerate((own_a, own_b, far_a, far_b)):
        normed[index * part:(index + 1) * part, :] = norm(ref[...].astype(jnp.float32), gain[...])
    allowed = lq[...] == lk[...]
    head_of = lax.broadcasted_iota(jnp.int32, (half, inner), 1) // HEAD
    acc[...] = jnp.zeros_like(acc)

    def quarter(step, carry):
        pltpu.make_async_copy(native, held.at[step], sems.at[step]).wait()

        def block(low, count):
            return held[step, :, low:low + count, :].reshape(slices * count, width)

        weight = block(0, rows)
        keyval = jnp.dot(normed[...], weight[:, inner:], preferred_element_type=jnp.float32).astype(jnp.bfloat16)
        query = jnp.dot(normed[:half, :], weight[:, :inner], preferred_element_type=jnp.float32)
        query = (query * (HEAD ** -0.5)).astype(jnp.bfloat16)
        key, value = keyval[:, :inner], keyval[:, inner:]
        stacked = jnp.concatenate(
            [jnp.where(head_of == head, query, jnp.zeros_like(query)) for head in range(heads)], axis=0
        )
        scores = lax.dot_general(stacked, key, (((1,), (1,)), ((), ())), preferred_element_type=jnp.float32)
        scores = jnp.where(jnp.concatenate([allowed] * heads, axis=0), scores, -jnp.inf)
        weights = jnp.exp(scores - jnp.max(scores, axis=-1, keepdims=True))
        total = jnp.sum(weights, axis=-1, keepdims=True)
        mixed = jnp.dot(weights.astype(jnp.bfloat16), value, preferred_element_type=jnp.float32) / total
        blended = mixed[:half]
        for head in range(1, heads):
            blended = jnp.where(head_of == head, mixed[head * half:(head + 1) * half], blended)
        blended = blended.astype(jnp.bfloat16)
        for side in range(2):
            update = jnp.dot(blended, block(rows + side * orows, orows), preferred_element_type=jnp.float32)
            update = update.astype(jnp.bfloat16).astype(jnp.float32)
            cols = slice(side * width, (side + 1) * width)
            acc[:, cols] += update
        return carry

    lax.fori_loop(0, quarters, quarter, 0)
    out_a[...] = (own_a[...].astype(jnp.float32) + acc[:part, :]).astype(jnp.bfloat16)
    out_b[...] = (own_b[...].astype(jnp.float32) + acc[part:, :]).astype(jnp.bfloat16)


def layer(lq, lk, gain, own_a, own_b, far_a, far_b, native, others):
    part, depth = own_a.shape
    quarters = others.shape[1] + 1
    vmem = pl.BlockSpec(memory_space=pltpu.VMEM)
    hbm = pl.BlockSpec(memory_space=pl.ANY)
    shape = jax.ShapeDtypeStruct((part, depth), jnp.bfloat16)
    return pl.pallas_call(
        layer_kernel,
        out_shape=(shape, shape),
        in_specs=[vmem] * 7 + [hbm] * 2,
        out_specs=(vmem, vmem),
        scratch_shapes=[
            pltpu.VMEM((quarters,) + native.shape, jnp.bfloat16),
            pltpu.VMEM((4 * part, depth), jnp.bfloat16),
            pltpu.VMEM((2 * part, depth), jnp.float32),
            pltpu.SemaphoreType.DMA((quarters,)),
        ],
        compiler_params=pltpu.CompilerParams(vmem_limit_bytes=48 << 20),
        cost_estimate=pl.CostEstimate(flops=2_600_000_000, bytes_accessed=14_000_000, transcendentals=524288),
        name="layer",
    )(lq, lk, gain, own_b, own_a, far_b, far_a, native, others)


def decode_kernel(gain, part_a, part_b, matrix, out):
    rows = jnp.concatenate([part_a[...], part_b[...]], axis=0).astype(jnp.float32)
    final = norm(rows, gain[...])
    for section in range(matrix.shape[0]):
        out[section] = lax.dot_general(
            final, matrix[section], (((1,), (1,)), ((), ())), preferred_element_type=jnp.float32
        ).astype(jnp.bfloat16)


def decode(gain, part_a, part_b, matrix):
    vmem = pl.BlockSpec(memory_space=pltpu.VMEM)
    return pl.pallas_call(
        decode_kernel,
        out_shape=jax.ShapeDtypeStruct((matrix.shape[0], 2 * part_a.shape[0], matrix.shape[1]), jnp.bfloat16),
        in_specs=[vmem] * 4,
        out_specs=vmem,
        compiler_params=pltpu.CompilerParams(vmem_limit_bytes=24 << 20),
        cost_estimate=pl.CostEstimate(flops=450_000_000, bytes_accessed=4_500_000, transcendentals=0),
        name="decode",
    )(gain, part_a, part_b, matrix)


def solution(mesh):
    sections, windows, bands = (mesh.shape[name] for name in ("section", "win", "dp"))
    fine = Mesh(np.asarray(mesh.devices).reshape(sections, windows // 16, 8, 2, bands), AXES)
    chips = windows // 2

    def place(section, window, chip):
        return (section * windows + window % windows) * bands + chip

    def send(value, route, sources):
        pairs = []
        for section in sources:
            for window in range(windows):
                for chip in range(bands):
                    target = route(section, window, chip)
                    if target is not None:
                        pairs.append((place(section, window, chip), place(*target)))
        return lax.ppermute(value, AXES, pairs)

    def to_other_core(value, sources):
        return send(value, lambda s, w, d: (s, w ^ 1, d), sources)

    def body(tokens, regions, norm_gain, qkv_weight, out_weight, final_gain, dec_weight):
        section = lax.axis_index("section")
        core = lax.axis_index("core")
        chip = lax.axis_index("dp")
        mine = lax.axis_index("y") * 2 + core
        depth = tokens.shape[-1]
        quad = tokens.shape[3]
        half = quad // 2
        micro = chip >> 1
        parity = (chip ^ (chip >> 1)) & 1
        width = qkv_weight.shape[2] * qkv_weight.shape[3]

        low = mine * (depth // 16)
        orows = out_weight.shape[1] // 16

        def slab(rows, outs):
            return jnp.concatenate([rows, outs[..., :width], outs[..., width:]], axis=-2)

        piece = slab(
            lax.dynamic_slice_in_dim(qkv_weight[0], low, depth // 16, 0).reshape(-1, width),
            lax.dynamic_slice_in_dim(out_weight[0], mine * orows, orows, 0),
        )
        column = lax.all_gather(piece, "dp", axis=0)
        rolled = lax.dynamic_slice_in_dim(jnp.concatenate([column, column], axis=0), chip + 1, bands - 1, 0)
        others = lax.all_gather(rolled, ("y", "core"), axis=0)
        qkv_weight, out_weight, dec_weight, tokens, regions, _ = lax.optimization_barrier(
            (qkv_weight, out_weight, dec_weight, tokens, regions, rolled)
        )
        native = slab(qkv_weight[0].reshape(16, depth // 16, width), out_weight[0].reshape(16, orows, 2 * width))
        last = sections - 1
        turned = dec_weight.T
        wide = turned.shape[0]
        strip = lax.dynamic_slice_in_dim(turned, core * (wide // 2), wide // 2, 0)
        strips = jnp.stack(
            [send(strip, lambda s, w, d: (last, w, d), (source,)) for source in range(last)]
        )
        matched = to_other_core(strips, (last,))
        strips = jnp.stack([jnp.where(core == 0, strips, matched), jnp.where(core == 0, matched, strips)], axis=1)
        matrix = jnp.concatenate([strips.reshape(last, wide, depth), turned[None]], axis=0)

        labels = regions[0, 0]
        labels = jnp.where(parity == core, labels, to_other_core(labels, range(sections)))
        labels = labels.reshape(2, 2, 2, half)
        labels = jnp.where(core == 0, labels, labels[::-1]).transpose(0, 2, 1, 3).reshape(-1)
        lk = labels[None, :]
        lq = labels[:quad * 2, None]

        even = chip % 2 == 0
        tokens = tokens[:, 0, 0]

        def first(flip):
            def route(s, w, d):
                return (s, (w // 2) * 2 + d // 2, chip_of(w % 2, d % 2 ^ flip))
            payload = jnp.where(even if flip == 0 else jnp.logical_not(even), tokens[0], tokens[1])
            return send(payload, route, (0,))

        near, far = first(0), first(1)
        band0 = jnp.where(micro == 0, near, far)
        band1 = jnp.where(micro == 0, far, near)
        own_a = jnp.concatenate([band0[:half], band1[:half]], axis=0)
        own_b = jnp.concatenate([band0[half:], band1[half:]], axis=0)

        def same(s, w, d):
            return (s + 1, w, d)

        def behind(s, w, d):
            window = (w // 2) * 2 + parity_of(d) - 1
            return (s + 1, (window % windows) // 2 * 2 + w % 2, chip_of(window % 2, d >> 1))

        for step in range(sections):
            far_a = to_other_core(own_a, (step,))
            far_b = to_other_core(own_b, (step,))
            out_a, out_b = layer(lq, lk, norm_gain, own_a, own_b, far_a, far_b, native, others)
            if step + 1 < sections:
                own_b = send(out_a, behind, (step,))
                own_a = send(out_b, same, (step,))
        values = decode(final_gain[None, :], out_a, out_b, matrix)

        values = values.reshape(sections, 2, 2, half, -1)
        flipped = micro == 1

        def home(flip):
            def route(s, w, d):
                return (s, (w // 2) * 2 + parity_of(d), 2 * (w % 2) + ((d >> 1) ^ flip))
            swap = flipped if flip == 0 else jnp.logical_not(flipped)
            return send(jnp.where(swap, values[:, :, 1], values[:, :, 0]), route, (last,))

        straight, crossed = home(0), home(1)
        result = jnp.stack(
            [jnp.where(even, straight, crossed), jnp.where(even, crossed, straight)], axis=1
        )
        shown = None
        for target in reversed(range(sections)):
            ahead = send(result[target, :, 0], lambda s, w, d: (target, w - 1, d), (last,))
            kept = result[target, :, 1]
            if target != last:
                kept = send(kept, lambda s, w, d: (target, w, d), (last,))
            here = jnp.concatenate([kept, ahead], axis=1)
            shown = here if shown is None else jnp.where(section == target, here, shown)
        return shown[:, None, None]

    return jax.shard_map(
        body,
        mesh=fine,
        in_specs=(
            P(None, WIN, "dp", None, None),
            P("section", WIN, None),
            P("section", None),
            P("section", None, None, "dp"),
            P("section", "dp", None),
            P(),
            P(None, "section"),
        ),
        out_specs=P(None, WIN, "dp", None, "section"),
        check_vma=False,
    )
```

```python
import jax
import jax.numpy as jnp
import numpy as np
from jax import lax
from jax.experimental import pallas as pl
from jax.experimental.pallas import tpu as pltpu
from jax.sharding import Mesh
from jax.sharding import PartitionSpec as P

HEAD = 64
AXES = ("section", "x", "y", "core", "dp")
WIN = ("x", "y", "core")


def chip_of(parity, micro):
    return 2 * micro + (parity ^ micro)


def parity_of(chip):
    return (chip ^ (chip >> 1)) & 1


def norm(values, gain):
    center = values - jnp.mean(values, axis=-1, keepdims=True)
    spread = jnp.mean(center * center, axis=-1, keepdims=True)
    return (center * lax.rsqrt(spread + 1e-05) * gain).astype(jnp.bfloat16)


def layer_kernel(lq, lk, gain, own_b, own_a, far_b, far_a, native, others, out_a, out_b, held, normed, acc, sems):
    quarters, slices, per, width = held.shape
    inner = width // 3
    heads = inner // HEAD
    rows = per * 3 // 4
    orows = per // 8
    part = own_a.shape[0]
    half = 2 * part
    copies = []
    for step in range(quarters):
        source = native.at[:slices] if step == 0 else others.at[:, step - 1]
        copies.append(pltpu.make_async_copy(source, held.at[step], sems.at[step]))
        copies[-1].start()
    for index, ref in enumerate((own_a, own_b, far_a, far_b)):
        normed[index * part:(index + 1) * part, :] = norm(ref[...].astype(jnp.float32), gain[...])
    allowed = lq[...] == lk[...]
    head_of = lax.broadcasted_iota(jnp.int32, (half, inner), 1) // HEAD
    acc[...] = jnp.zeros_like(acc)

    def quarter(step, carry):
        pltpu.make_async_copy(native.at[:slices], held.at[step], sems.at[step]).wait()

        def block(low, count):
            return held[step, :, low:low + count, :].reshape(slices * count, width)

        weight = block(0, rows)
        keyval = jnp.dot(normed[...], weight[:, inner:], preferred_element_type=jnp.float32).astype(jnp.bfloat16)
        query = jnp.dot(normed[:half, :], weight[:, :inner], preferred_element_type=jnp.float32)
        query = (query * (HEAD ** -0.5)).astype(jnp.bfloat16)
        key, value = keyval[:, :inner], keyval[:, inner:]
        stacked = jnp.concatenate(
            [jnp.where(head_of == head, query, jnp.zeros_like(query)) for head in range(heads)], axis=0
        )
        scores = lax.dot_general(stacked, key, (((1,), (1,)), ((), ())), preferred_element_type=jnp.float32)
        scores = jnp.where(jnp.concatenate([allowed] * heads, axis=0), scores, -jnp.inf)
        weights = jnp.exp(scores - jnp.max(scores, axis=-1, keepdims=True))
        total = jnp.sum(weights, axis=-1, keepdims=True)
        mixed = jnp.dot(weights.astype(jnp.bfloat16), value, preferred_element_type=jnp.float32) / total
        blended = mixed[:half]
        for head in range(1, heads):
            blended = jnp.where(head_of == head, mixed[head * half:(head + 1) * half], blended)
        blended = blended.astype(jnp.bfloat16)
        for side in range(2):
            update = jnp.dot(blended, block(rows + side * orows, orows), preferred_element_type=jnp.float32)
            update = update.astype(jnp.bfloat16).astype(jnp.float32)
            cols = slice(side * width, (side + 1) * width)
            acc[:, cols] += update
        return carry

    lax.fori_loop(0, quarters, quarter, 0)
    out_a[...] = (own_a[...].astype(jnp.float32) + acc[:part, :]).astype(jnp.bfloat16)
    out_b[...] = (own_b[...].astype(jnp.float32) + acc[part:, :]).astype(jnp.bfloat16)


def layer(lq, lk, gain, own_a, own_b, far_a, far_b, native, others):
    part, depth = own_a.shape
    quarters = others.shape[1] + 1
    vmem = pl.BlockSpec(memory_space=pltpu.VMEM)
    hbm = pl.BlockSpec(memory_space=pl.ANY)
    shape = jax.ShapeDtypeStruct((part, depth), jnp.bfloat16)
    return pl.pallas_call(
        layer_kernel,
        out_shape=(shape, shape),
        in_specs=[vmem] * 7 + [hbm] * 2,
        out_specs=(vmem, vmem),
        scratch_shapes=[
            pltpu.VMEM((quarters, others.shape[0]) + native.shape[1:], jnp.bfloat16),
            pltpu.VMEM((4 * part, depth), jnp.bfloat16),
            pltpu.VMEM((2 * part, depth), jnp.float32),
            pltpu.SemaphoreType.DMA((quarters,)),
        ],
        compiler_params=pltpu.CompilerParams(vmem_limit_bytes=51 << 20),
        cost_estimate=pl.CostEstimate(flops=2_600_000_000, bytes_accessed=14_000_000, transcendentals=524288),
        name="layer",
    )(lq, lk, gain, own_b, own_a, far_b, far_a, native, others)


def decode_kernel(gain, part_a, part_b, matrix, out):
    rows = jnp.concatenate([part_a[...], part_b[...]], axis=0).astype(jnp.float32)
    final = norm(rows, gain[...])
    for section in range(matrix.shape[0]):
        out[section] = lax.dot_general(
            final, matrix[section], (((1,), (1,)), ((), ())), preferred_element_type=jnp.float32
        ).astype(jnp.bfloat16)


def decode(gain, part_a, part_b, matrix):
    vmem = pl.BlockSpec(memory_space=pltpu.VMEM)
    return pl.pallas_call(
        decode_kernel,
        out_shape=jax.ShapeDtypeStruct((matrix.shape[0], 2 * part_a.shape[0], matrix.shape[1]), jnp.bfloat16),
        in_specs=[vmem] * 4,
        out_specs=vmem,
        compiler_params=pltpu.CompilerParams(vmem_limit_bytes=24 << 20),
        cost_estimate=pl.CostEstimate(flops=450_000_000, bytes_accessed=4_500_000, transcendentals=0),
        name="decode",
    )(gain, part_a, part_b, matrix)


def solution(mesh):
    sections, windows, bands = (mesh.shape[name] for name in ("section", "win", "dp"))
    fine = Mesh(np.asarray(mesh.devices).reshape(sections, windows // 16, 8, 2, bands), AXES)
    chips = windows // 2

    def place(section, window, chip):
        return (section * windows + window % windows) * bands + chip

    def send(value, route, sources):
        pairs = []
        for section in sources:
            for window in range(windows):
                for chip in range(bands):
                    target = route(section, window, chip)
                    if target is not None:
                        pairs.append((place(section, window, chip), place(*target)))
        return lax.ppermute(value, AXES, pairs)

    def to_other_core(value, sources):
        return send(value, lambda s, w, d: (s, w ^ 1, d), sources)

    def body(tokens, regions, norm_gain, qkv_weight, out_weight, final_gain, dec_weight):
        section = lax.axis_index("section")
        core = lax.axis_index("core")
        chip = lax.axis_index("dp")
        mine = lax.axis_index("y") * 2 + core
        depth = tokens.shape[-1]
        quad = tokens.shape[3]
        half = quad // 2
        micro = chip >> 1
        parity = (chip ^ (chip >> 1)) & 1
        width = qkv_weight.shape[2] * qkv_weight.shape[3]

        low = mine * (depth // 16)
        orows = out_weight.shape[1] // 16

        def slab(rows, outs):
            return jnp.concatenate([rows, outs[..., :width], outs[..., width:]], axis=-2)

        piece = slab(
            lax.dynamic_slice_in_dim(qkv_weight[0], low, depth // 16, 0).reshape(-1, width),
            lax.dynamic_slice_in_dim(out_weight[0], mine * orows, orows, 0),
        )
        column = lax.all_gather(piece, "dp", axis=0)
        rolled = lax.dynamic_slice_in_dim(jnp.concatenate([column, column], axis=0), chip + 1, bands - 1, 0)
        others = lax.all_gather(rolled, ("y", "core"), axis=0)
        qkv_weight, out_weight, dec_weight, tokens, regions, _ = lax.optimization_barrier(
            (qkv_weight, out_weight, dec_weight, tokens, regions, rolled)
        )
        native = slab(qkv_weight[0].reshape(16, depth // 16, width), out_weight[0].reshape(16, orows, 2 * width))
        native = jnp.pad(native, ((0, 4), (0, 0), (0, 0)))
        last = sections - 1
        turned = dec_weight.T
        wide = turned.shape[0]
        strip = lax.dynamic_slice_in_dim(turned, core * (wide // 2), wide // 2, 0)
        strips = jnp.stack(
            [send(strip, lambda s, w, d: (last, w, d), (source,)) for source in range(last)]
        )
        matched = to_other_core(strips, (last,))
        strips = jnp.stack([jnp.where(core == 0, strips, matched), jnp.where(core == 0, matched, strips)], axis=1)
        matrix = jnp.concatenate([strips.reshape(last, wide, depth), turned[None]], axis=0)

        labels = regions[0, 0]
        labels = jnp.where(parity == core, labels, to_other_core(labels, range(sections)))
        labels = labels.reshape(2, 2, 2, half)
        labels = jnp.where(core == 0, labels, labels[::-1]).transpose(0, 2, 1, 3).reshape(-1)
        lk = labels[None, :]
        lq = labels[:quad * 2, None]

        even = chip % 2 == 0
        tokens = tokens[:, 0, 0]

        def first(flip):
            def route(s, w, d):
                return (s, (w // 2) * 2 + d // 2, chip_of(w % 2, d % 2 ^ flip))
            payload = jnp.where(even if flip == 0 else jnp.logical_not(even), tokens[0], tokens[1])
            return send(payload, route, (0,))

        near, far = first(0), first(1)
        band0 = jnp.where(micro == 0, near, far)
        band1 = jnp.where(micro == 0, far, near)
        own_a = jnp.concatenate([band0[:half], band1[:half]], axis=0)
        own_b = jnp.concatenate([band0[half:], band1[half:]], axis=0)

        def same(s, w, d):
            return (s + 1, w, d)

        def behind(s, w, d):
            window = (w // 2) * 2 + parity_of(d) - 1
            return (s + 1, (window % windows) // 2 * 2 + w % 2, chip_of(window % 2, d >> 1))

        for step in range(sections):
            far_a = to_other_core(own_a, (step,))
            far_b = to_other_core(own_b, (step,))
            out_a, out_b = layer(lq, lk, norm_gain, own_a, own_b, far_a, far_b, native, others)
            if step + 1 < sections:
                own_b = send(out_a, behind, (step,))
                own_a = send(out_b, same, (step,))
        values = decode(final_gain[None, :], out_a, out_b, matrix)

        values = values.reshape(sections, 2, 2, half, -1)
        flipped = micro == 1

        def home(flip):
            def route(s, w, d):
                return (s, (w // 2) * 2 + parity_of(d), 2 * (w % 2) + ((d >> 1) ^ flip))
            swap = flipped if flip == 0 else jnp.logical_not(flipped)
            return send(jnp.where(swap, values[:, :, 1], values[:, :, 0]), route, (last,))

        straight, crossed = home(0), home(1)
        result = jnp.stack(
            [jnp.where(even, straight, crossed), jnp.where(even, crossed, straight)], axis=1
        )
        shown = None
        for target in reversed(range(sections)):
            ahead = send(result[target, :, 0], lambda s, w, d: (target, w - 1, d), (last,))
            kept = result[target, :, 1]
            if target != last:
                kept = send(kept, lambda s, w, d: (target, w, d), (last,))
            here = jnp.concatenate([kept, ahead], axis=1)
            shown = here if shown is None else jnp.where(section == target, here, shown)
        return shown[:, None, None]

    return jax.shard_map(
        body,
        mesh=fine,
        in_specs=(
            P(None, WIN, "dp", None, None),
            P("section", WIN, None),
            P("section", None),
            P("section", None, None, "dp"),
            P("section", "dp", None),
            P(),
            P(None, "section"),
        ),
        out_specs=P(None, WIN, "dp", None, "section"),
        check_vma=False,
    )
```

```python
import jax
import jax.numpy as jnp
import numpy as np
from jax import lax
from jax.experimental import pallas as pl
from jax.experimental.pallas import tpu as pltpu
from jax.sharding import Mesh
from jax.sharding import PartitionSpec as P

HEAD = 64
AXES = ("section", "x", "y", "core", "dp")
WIN = ("x", "y", "core")


def chip_of(parity, micro):
    return 2 * micro + (parity ^ micro)


def parity_of(chip):
    return (chip ^ (chip >> 1)) & 1


def norm(values, gain):
    center = values - jnp.mean(values, axis=-1, keepdims=True)
    spread = jnp.mean(center * center, axis=-1, keepdims=True)
    return (center * lax.rsqrt(spread + 1e-05) * gain).astype(jnp.bfloat16)


def layer_kernel(lq, lk, gain, own_b, own_a, far_b, far_a, native, others, out_a, out_b, held, normed, acc, sems):
    quarters, slices, per, width = held.shape
    inner = width // 3
    heads = inner // HEAD
    rows = per * 3 // 4
    orows = per // 8
    part = own_a.shape[0]
    half = 2 * part
    copies = []
    for step in range(quarters):
        source = native.at[:slices] if step == 0 else others.at[:, step - 1]
        copies.append(pltpu.make_async_copy(source, held.at[step], sems.at[step]))
        copies[-1].start()
    for index, ref in enumerate((own_a, own_b, far_a, far_b)):
        normed[index * part:(index + 1) * part, :] = norm(ref[...].astype(jnp.float32), gain[...])
    allowed = lq[...] == lk[...]
    head_of = lax.broadcasted_iota(jnp.int32, (half, inner), 1) // HEAD
    acc[...] = jnp.zeros_like(acc)

    def quarter(step, carry):
        pltpu.make_async_copy(native.at[:slices], held.at[step], sems.at[step]).wait()

        def block(low, count):
            return held[step, :, low:low + count, :].reshape(slices * count, width)

        weight = block(0, rows)
        keyval = jnp.dot(normed[...], weight[:, inner:], preferred_element_type=jnp.float32).astype(jnp.bfloat16)
        query = jnp.dot(normed[:half, :], weight[:, :inner], preferred_element_type=jnp.float32)
        query = (query * (HEAD ** -0.5)).astype(jnp.bfloat16)
        key, value = keyval[:, :inner], keyval[:, inner:]
        stacked = jnp.concatenate(
            [jnp.where(head_of == head, query, jnp.zeros_like(query)) for head in range(heads)], axis=0
        )
        scores = lax.dot_general(stacked, key, (((1,), (1,)), ((), ())), preferred_element_type=jnp.float32)
        scores = jnp.where(jnp.concatenate([allowed] * heads, axis=0), scores, -jnp.inf)
        weights = jnp.exp(scores - jnp.max(scores, axis=-1, keepdims=True))
        total = jnp.sum(weights, axis=-1, keepdims=True)
        mixed = jnp.dot(weights.astype(jnp.bfloat16), value, preferred_element_type=jnp.float32) / total
        blended = mixed[:half]
        for head in range(1, heads):
            blended = jnp.where(head_of == head, mixed[head * half:(head + 1) * half], blended)
        blended = blended.astype(jnp.bfloat16)
        for side in range(2):
            update = jnp.dot(blended, block(rows + side * orows, orows), preferred_element_type=jnp.float32)
            update = update.astype(jnp.bfloat16).astype(jnp.float32)
            cols = slice(side * width, (side + 1) * width)
            acc[:, cols] += update
        return carry

    lax.fori_loop(0, quarters, quarter, 0)
    out_a[...] = (own_a[...].astype(jnp.float32) + acc[:part, :]).astype(jnp.bfloat16)
    out_b[...] = (own_b[...].astype(jnp.float32) + acc[part:, :]).astype(jnp.bfloat16)


def layer(lq, lk, gain, own_a, own_b, far_a, far_b, native, others):
    part, depth = own_a.shape
    quarters = others.shape[1] + 1
    vmem = pl.BlockSpec(memory_space=pltpu.VMEM)
    hbm = pl.BlockSpec(memory_space=pl.ANY)
    shape = jax.ShapeDtypeStruct((part, depth), jnp.bfloat16)
    return pl.pallas_call(
        layer_kernel,
        out_shape=(shape, shape),
        in_specs=[vmem] * 7 + [hbm] * 2,
        out_specs=(vmem, vmem),
        scratch_shapes=[
            pltpu.VMEM((quarters, others.shape[0]) + native.shape[1:], jnp.bfloat16),
            pltpu.VMEM((4 * part, depth), jnp.bfloat16),
            pltpu.VMEM((2 * part, depth), jnp.float32),
            pltpu.SemaphoreType.DMA((quarters,)),
        ],
        compiler_params=pltpu.CompilerParams(vmem_limit_bytes=48 << 20),
        cost_estimate=pl.CostEstimate(flops=2_600_000_000, bytes_accessed=14_000_000, transcendentals=524288),
        name="layer",
    )(lq, lk, gain, own_b, own_a, far_b, far_a, native, others)


def decode_kernel(gain, part_a, part_b, matrix, out):
    rows = jnp.concatenate([part_a[...], part_b[...]], axis=0).astype(jnp.float32)
    final = norm(rows, gain[...])
    for section in range(matrix.shape[0]):
        out[section] = lax.dot_general(
            final, matrix[section], (((1,), (1,)), ((), ())), preferred_element_type=jnp.float32
        ).astype(jnp.bfloat16)


def decode(gain, part_a, part_b, matrix):
    vmem = pl.BlockSpec(memory_space=pltpu.VMEM)
    return pl.pallas_call(
        decode_kernel,
        out_shape=jax.ShapeDtypeStruct((matrix.shape[0], 2 * part_a.shape[0], matrix.shape[1]), jnp.bfloat16),
        in_specs=[vmem] * 4,
        out_specs=vmem,
        compiler_params=pltpu.CompilerParams(vmem_limit_bytes=24 << 20),
        cost_estimate=pl.CostEstimate(flops=450_000_000, bytes_accessed=4_500_000, transcendentals=0),
        name="decode",
    )(gain, part_a, part_b, matrix)


def solution(mesh):
    sections, windows, bands = (mesh.shape[name] for name in ("section", "win", "dp"))
    fine = Mesh(np.asarray(mesh.devices).reshape(sections, windows // 16, 8, 2, bands), AXES)
    chips = windows // 2

    def place(section, window, chip):
        return (section * windows + window % windows) * bands + chip

    def send(value, route, sources):
        pairs = []
        for section in sources:
            for window in range(windows):
                for chip in range(bands):
                    target = route(section, window, chip)
                    if target is not None:
                        pairs.append((place(section, window, chip), place(*target)))
        return lax.ppermute(value, AXES, pairs)

    def to_other_core(value, sources):
        return send(value, lambda s, w, d: (s, w ^ 1, d), sources)

    def body(tokens, regions, norm_gain, qkv_weight, out_weight, final_gain, dec_weight):
        section = lax.axis_index("section")
        core = lax.axis_index("core")
        chip = lax.axis_index("dp")
        mine = lax.axis_index("y") * 2 + core
        depth = tokens.shape[-1]
        quad = tokens.shape[3]
        half = quad // 2
        micro = chip >> 1
        parity = (chip ^ (chip >> 1)) & 1
        width = qkv_weight.shape[2] * qkv_weight.shape[3]

        low = mine * (depth // 16)
        orows = out_weight.shape[1] // 16

        def slab(rows, outs):
            return jnp.concatenate([rows, outs[..., :width], outs[..., width:]], axis=-2)

        piece = slab(
            lax.dynamic_slice_in_dim(qkv_weight[0], low, depth // 16, 0).reshape(-1, width),
            lax.dynamic_slice_in_dim(out_weight[0], mine * orows, orows, 0),
        )
        column = lax.all_gather(piece, "dp", axis=0)
        rolled = lax.dynamic_slice_in_dim(jnp.concatenate([column, column], axis=0), chip + 1, bands - 1, 0)
        others = lax.all_gather(rolled, ("y", "core"), axis=0)
        qkv_weight, out_weight, dec_weight, tokens, regions, _ = lax.optimization_barrier(
            (qkv_weight, out_weight, dec_weight, tokens, regions, rolled)
        )
        native = slab(qkv_weight[0].reshape(16, depth // 16, width), out_weight[0].reshape(16, orows, 2 * width))
        native = jnp.pad(native, ((0, 4), (0, 0), (0, 0)))
        last = sections - 1
        turned = dec_weight.T
        wide = turned.shape[0]
        strip = lax.dynamic_slice_in_dim(turned, core * (wide // 2), wide // 2, 0)
        strips = jnp.stack(
            [send(strip, lambda s, w, d: (last, w, d), (source,)) for source in range(last)]
        )
        matched = to_other_core(strips, (last,))
        strips = jnp.stack([jnp.where(core == 0, strips, matched), jnp.where(core == 0, matched, strips)], axis=1)
        matrix = jnp.concatenate([strips.reshape(last, wide, depth), turned[None]], axis=0)

        labels = regions[0, 0]
        labels = jnp.where(parity == core, labels, to_other_core(labels, range(sections)))
        labels = labels.reshape(2, 2, 2, half)
        labels = jnp.where(core == 0, labels, labels[::-1]).transpose(0, 2, 1, 3).reshape(-1)
        lk = labels[None, :]
        lq = labels[:quad * 2, None]

        even = chip % 2 == 0
        tokens = tokens[:, 0, 0]

        def first(flip):
            def route(s, w, d):
                return (s, (w // 2) * 2 + d // 2, chip_of(w % 2, d % 2 ^ flip))
            payload = jnp.where(even if flip == 0 else jnp.logical_not(even), tokens[0], tokens[1])
            return send(payload, route, (0,))

        near, far = first(0), first(1)
        band0 = jnp.where(micro == 0, near, far)
        band1 = jnp.where(micro == 0, far, near)
        own_a = jnp.concatenate([band0[:half], band1[:half]], axis=0)
        own_b = jnp.concatenate([band0[half:], band1[half:]], axis=0)

        def same(s, w, d):
            return (s + 1, w, d)

        def behind(s, w, d):
            window = (w // 2) * 2 + parity_of(d) - 1
            return (s + 1, (window % windows) // 2 * 2 + w % 2, chip_of(window % 2, d >> 1))

        for step in range(sections):
            far_a = to_other_core(own_a, (step,))
            far_b = to_other_core(own_b, (step,))
            out_a, out_b = layer(lq, lk, norm_gain, own_a, own_b, far_a, far_b, native, others)
            if step + 1 < sections:
                own_b = send(out_a, behind, (step,))
                own_a = send(out_b, same, (step,))
        values = decode(final_gain[None, :], out_a, out_b, matrix)

        values = values.reshape(sections, 2, 2, half, -1)
        flipped = micro == 1

        def home(flip):
            def route(s, w, d):
                return (s, (w // 2) * 2 + parity_of(d), 2 * (w % 2) + ((d >> 1) ^ flip))
            swap = flipped if flip == 0 else jnp.logical_not(flipped)
            return send(jnp.where(swap, values[:, :, 1], values[:, :, 0]), route, (last,))

        straight, crossed = home(0), home(1)
        result = jnp.stack(
            [jnp.where(even, straight, crossed), jnp.where(even, crossed, straight)], axis=1
        )
        shown = None
        for target in reversed(range(sections)):
            ahead = send(result[target, :, 0], lambda s, w, d: (target, w - 1, d), (last,))
            kept = result[target, :, 1]
            if target != last:
                kept = send(kept, lambda s, w, d: (target, w, d), (last,))
            here = jnp.concatenate([kept, ahead], axis=1)
            shown = here if shown is None else jnp.where(section == target, here, shown)
        return shown[:, None, None]

    return jax.shard_map(
        body,
        mesh=fine,
        in_specs=(
            P(None, WIN, "dp", None, None),
            P("section", WIN, None),
            P("section", None),
            P("section", None, None, "dp"),
            P("section", "dp", None),
            P(),
            P(None, "section"),
        ),
        out_specs=P(None, WIN, "dp", None, "section"),
        check_vma=False,
    )
```
